256 devices in a mesh: layer: 4 (over z_lo), latent: 64 (over y, z_hi, x, core).
Axes of the slice: x: 4, y: 4, z: 8 (z_hi: 2, z_lo: 4; z = z_hi * 4 + z_lo), core: 2. Of those that a mesh axis runs over, the one named last changes fastest.
Arguments:
- acts: float32 [4, 512, 2304], P('layer', 'latent'), may hold values from -6 to 6
- w_enc: float32 [4, 2304, 16384], P('layer', None, 'latent'), may hold values from -0.0625 to 0.0625
- b_enc: float32 [16384], P('latent'), may hold values from -3 to 3
- w_dec: float32 [16384, 4, 2304], P('latent', 'layer'), may hold values from -0.046875 to 0.046875
- b_dec: float32 [4, 2304], P('layer'), may hold values from -3 to 3
Outputs:
- grad_enc: float32 [4, 2304, 16384], P('layer', None, 'latent')
- grad_benc: float32 [16384], P('latent')
The draws below stay inside these ranges and needn't reach their ends.
All inputs are finite; a program needn't handle non-finite values.
Results may differ from the reference program's by a relative error of at most 0.000076.
Values sent between devices are 32-bit elements; how exact they have to be, the bound alone decides.
A program may use at most 64 MiB of HBM per device.

```python
import jax
import jax.numpy as jnp
from jax import lax

D = 2304
H = 16384
LAYERS = 4
TOKENS = 512


def shard_levels(rng, dims, split, least, high):
    factor_of, own = 1.0, jax.random.fold_in(rng, 6)
    for axis_at, blocks in split:
        steps = jnp.exp(jax.random.uniform(jax.random.fold_in(own, axis_at), (blocks,), jnp.float32, least / len(split), high / len(split)))
        factor_of = factor_of * jnp.repeat(steps, dims[axis_at] // blocks).reshape([-1 if axis == axis_at else 1 for axis in range(len(dims))])
    return factor_of


def bell_draw(rng, shape, width, most, cuts=(), dtype=jnp.bfloat16):
    values = jax.random.normal(rng, shape, jnp.float32) * width
    if len(cuts) > 0:
        values = shard_levels(rng, shape, cuts, -0.22, 0.18) * values
    return jnp.clip(values, min=-most, max=most).astype(dtype)


def setup_inputs(seed: int = 0) -> dict:
    key_list = jax.random.split(jax.random.key(seed), 6)
    return {
        "acts": bell_draw(key_list[0], (LAYERS, TOKENS, D), 1.0, 6.0, ((0, 4), (1, 64)), jnp.float32),
        "w_enc": bell_draw(key_list[1], (LAYERS, D, H), (LAYERS * D) ** -0.5, 0.0625, ((0, 4), (2, 64)), jnp.float32),
        "b_enc": bell_draw(key_list[2], (H,), 0.5, 3.0, ((0, 64),), jnp.float32),
        "w_dec": bell_draw(key_list[3], (H, LAYERS, D), H ** -0.5, 0.046875, ((0, 64), (1, 4)), jnp.float32),
        "b_dec": bell_draw(key_list[4], (LAYERS, D), 0.5, 3.0, ((0, 4),), jnp.float32),
    }


SHARP = 4.0

def reference(acts, w_enc, b_enc, w_dec, b_dec):
    high = lax.Precision.HIGHEST
    pre = jnp.einsum('ltd,ldh->th', acts, w_enc, precision=high) + b_enc[None, :]
    codes = jax.nn.softplus(SHARP * pre) / SHARP
    recon = jnp.einsum('th,hld->ltd', codes, w_dec, precision=high) + b_dec[:, None, :]
    resid = recon - acts
    dec_norm = lax.optimization_barrier(jnp.sum(jnp.sqrt(lax.optimization_barrier(jnp.sum(w_dec * w_dec, axis=2))), axis=1))
    code_grad = jnp.einsum('ltd,hld->th', resid, w_dec, precision=high) + dec_norm[None, :]
    pre_grad = code_grad * jax.nn.sigmoid(SHARP * pre)
    grad_enc = jnp.einsum('ltd,th->ldh', acts, pre_grad, precision=high)
    grad_benc = lax.optimization_barrier(jnp.sum(pre_grad, axis=0))
    return (grad_enc, grad_benc)
```

```python
import functools

import jax
import jax.numpy as jnp
from jax import lax
from jax.experimental import pallas as pl
from jax.experimental.pallas import tpu as pltpu
from jax.sharding import PartitionSpec as P

SHARP = 4.0
MESH = pl.DeviceIdType.MESH
F32 = jnp.float32
BF16 = jnp.bfloat16

STEPS = (0, 1, -1, 2)
UNIT = 8
CHUNK = 64


def split(value):
    high = value.astype(BF16)
    return high, (value - high.astype(F32)).astype(BF16)


def softplus_and_sigmoid(pre):
    x = SHARP * pre
    e = jnp.exp(-jnp.abs(x))
    codes = (jnp.maximum(x, 0.0) + jnp.log1p(e)) / SHARP
    inv = 1.0 / (1.0 + e)
    return codes, jnp.where(x >= 0, inv, e * inv)


def kernel(
    acts_hbm,
    wenc_hbm,
    wdec_hbm,
    bdec_ref,
    benc_ref,
    grad_hbm,
    gbias_ref,
    acts,
    acts_sib,
    resid,
    wenc,
    wdec,
    wenc_h,
    wenc_l,
    wdec_h,
    wdec_l,
    bias,
    norms,
    recon,
    row_sum,
    far_a,
    far_b,
    from_up,
    from_down,
    first_in,
    plane_out,
    plane_in,
    part,
    near_in,
    inner_out,
    far_in,
    outer_out,
    sig,
    pg,
    pg_in,
    acts_th,
    acts_tl,
    grad_buf,
    ssem,
    rsem,
    lsem,
):
    layer = lax.axis_index("layer")
    place = lax.axis_index("latent")
    core = lax.rem(place, 2)
    x = lax.rem(place // 2, 4)
    z_hi = lax.rem(place // 8, 2)
    y = place // 16

    def device(dx, dy, dz, dc):
        nx = lax.rem(x + dx + 4, 4)
        ny = lax.rem(y + dy + 4, 4)
        nz = lax.rem(z_hi + dz, 2)
        nc = lax.rem(core + dc, 2)
        return (layer, ((ny * 2 + nz) * 4 + nx) * 2 + nc)

    def first(d):
        return device(d * (1 - core), d * core, 0, 0)

    def second(d):
        return device(d * core, d * (1 - core), 0, 0)

    other_plane = device(0, 0, 1, 0)
    sibling = device(0, 0, 0, 1)
    upper = layer // 2
    inner = lax.rem(layer + upper, 2)
    toward = 1 - 2 * upper
    far = (layer + toward, place)
    near = (layer - toward, place)

    state = {"next": 0}
    sent = []

    def copy_to(src, dst, target, index=None):
        if index is None:
            index = state["next"]
            state["next"] += 1
        return pltpu.make_async_remote_copy(
            src_ref=src,
            dst_ref=dst,
            send_sem=ssem.at[index],
            recv_sem=rsem.at[index],
            device_id=target,
            device_id_type=MESH,
        )

    def send(src, dst, target):
        copy = copy_to(src, dst, target)
        copy.start()
        sent.append(copy)
        return copy

    load_acts = pltpu.make_async_copy(acts_hbm.at[0], acts.at[pl.ds(0, UNIT)], lsem.at[0])
    load_enc = pltpu.make_async_copy(wenc_hbm.at[0], wenc.at[0], lsem.at[1])
    load_dec = pltpu.make_async_copy(wdec_hbm, wdec.at[0], lsem.at[2])
    load_acts.start()
    load_enc.start()
    load_dec.start()

    barrier = pltpu.get_barrier_semaphore()
    partners = [first(1), first(-1), first(2), second(1), second(-1), other_plane, sibling, far]
    for partner in partners:
        pl.semaphore_signal(barrier, inc=1, device_id=partner, device_id_type=MESH)

    @pl.when(inner == 1)
    def _():
        pl.semaphore_signal(barrier, inc=1, device_id=near, device_id_type=MESH)

    pl.semaphore_wait(barrier, len(partners) + inner)

    def row(plane, b, a):
        return ((plane * 4 + b) * 4 + a) * UNIT

    def rows(ref, start, count):
        return ref.at[pl.ds(start, count)]

    def gather_first(ref, plane):
        own = rows(ref, row(plane, 0, 0), UNIT)
        return [
            send(own, rows(ref, row(plane, 0, 2), UNIT), first(1)),
            send(own, rows(ref, row(plane, 0, 1), UNIT), first(-1)),
            send(own, rows(ref, row(plane, 0, 3), UNIT), first(2)),
        ]

    def gather_second(ref, plane):
        half = 2 * UNIT
        own = row(plane, 0, 0)
        up = row(plane, 2, 0)
        down = row(plane, 1, 0)
        up0 = send(rows(ref, own, half), rows(ref, up, half), second(1))
        down1 = send(rows(ref, own + half, half), rows(ref, down + half, half), second(-1))
        up1 = send(rows(ref, own + half, half), rows(ref, up + half, half), second(1))
        down0 = send(rows(ref, own, half), rows(ref, down, half), second(-1))
        return up0, down1, up1, down0

    def gather_forward(ref, plane, copies):
        half = 2 * UNIT
        up0, down1, up1, down0 = copies
        last = row(plane, 3, 0)
        up0.wait_recv()
        fwd0 = send(rows(ref, row(plane, 2, 0), half), rows(ref, last, half), second(1))
        down1.wait_recv()
        fwd1 = send(rows(ref, row(plane, 1, 0) + half, half), rows(ref, last + half, half), second(-1))
        return up1, down0, fwd0, fwd1

    def wait_all(copies):
        for copy in copies:
            copy.wait_recv()

    def start_gather(ref):
        to_plane = send(rows(ref, 0, UNIT), rows(ref, row(1, 0, 0), UNIT), other_plane)
        return to_plane, gather_first(ref, 0)

    def split_weights(slot):
        def enc(i, _):
            at = pl.ds(pl.multiple_of(i * 256, 256), 256)
            high, low = split(wenc[slot, at, :])
            wenc_h[at, slot * 256 : (slot + 1) * 256] = high
            wenc_l[at, slot * 256 : (slot + 1) * 256] = low
            return 0

        lax.fori_loop(0, 9, enc, 0)

    def split_decoder(slot):
        def dec(i, _):
            at = pl.ds(pl.multiple_of(i * 32, 32), 32)
            to = pl.ds(pl.multiple_of(slot * 256 + i * 32, 32), 32)
            high, low = split(wdec[slot, at, :])
            wdec_h[to, :] = high
            wdec_l[to, :] = low
            return 0

        lax.fori_loop(0, 8, dec, 0)
        square = wdec[slot] * wdec[slot]
        total = lax.dot_general(
            jnp.ones((8, square.shape[1]), F32),
            square,
            (((1,), (1,)), ((), ())),
            precision=lax.Precision.HIGHEST,
            preferred_element_type=F32,
        )
        norms[:, slot * 256 : (slot + 1) * 256] = jnp.sqrt(total)

    def product(left, right_h, right_l, dims):
        high, low = split(left)
        count = left.shape[0]
        both = lax.dot_general(jnp.concatenate([high, low], axis=0), right_h, dims, preferred_element_type=F32)
        cross = lax.dot_general(high, right_l, dims, preferred_element_type=F32)
        return both[:count] + (both[count:] + cross)

    def sum_index(phase, chunk):
        return state["sum"] + phase * 3 * (256 // CHUNK) + chunk * 3

    def sum_start(phase, chunk):
        at = pl.ds(chunk * CHUNK, CHUNK)
        index = sum_index(phase, chunk)

        @pl.when(inner == 0)
        def _():
            copy_to(part.at[phase, at], near_in.at[phase, at], far, index).start()

    def sum_middle(phase, chunk):
        at = pl.ds(chunk * CHUNK, CHUNK)
        index = sum_index(phase, chunk)

        @pl.when(inner == 1)
        def _():
            copy_to(part.at[phase, at], near_in.at[phase, at], far, index).wait_recv()
            inner_out[phase, at] = part[phase, at] + near_in[phase, at]
            copy_to(inner_out.at[phase, at], far_in.at[phase, at], far, index + 1).start()

    def sum_finish(phase, chunk):
        at = pl.ds(chunk * CHUNK, CHUNK)
        index = sum_index(phase, chunk)
        copy_to(inner_out.at[phase, at], far_in.at[phase, at], far, index + 1).wait_recv()

        @pl.when(inner == 1)
        def _():
            outer_out[phase, at] = part[phase, at] + far_in[phase, at]
            pltpu.make_async_remote_copy(
                src_ref=outer_out.at[phase, at],
                dst_ref=far_in.at[phase, at],
                send_sem=ssem.at[index + 2],
                recv_sem=rsem.at[index + 1],
                device_id=near,
                device_id_type=MESH,
            ).start()
            inner_out_value = inner_out[phase, at]
            sig[at] = inner_out_value + far_in[phase, at]

        @pl.when(inner == 0)
        def _():
            sig[at] = part[phase, at] + far_in[phase, at]

    def sum_drain(phase, chunk):
        at = pl.ds(chunk * CHUNK, CHUNK)
        index = sum_index(phase, chunk)

        @pl.when(inner == 0)
        def _():
            copy_to(part.at[phase, at], near_in.at[phase, at], far, index).wait_send()

        @pl.when(inner == 1)
        def _():
            copy_to(inner_out.at[phase, at], far_in.at[phase, at], far, index + 1).wait_send()
            copy_to(outer_out.at[phase, at], far_in.at[phase, at], near, index + 2).wait_send()

    state["sum"] = 0
    state["next"] = 2 * 3 * (256 // CHUNK)
    chunks = range(256 // CHUNK)
    plain = (((1,), (0,)), ((), ()))
    turned = (((1,), (1,)), ((), ()))

    load_acts.wait()
    to_plane, own_first = start_gather(acts)
    load_enc.wait()
    swap_enc = send(wenc.at[0], wenc.at[1], sibling)
    load_dec.wait()
    swap_dec = send(wdec.at[0], wdec.at[1], sibling)
    wait_all(own_first)
    own_second = gather_second(acts, 0)
    split_weights(0)
    to_plane.wait_recv()
    other_first = gather_first(acts, 1)
    own_rest = gather_forward(acts, 0, own_second)
    wait_all(other_first)
    other_second = gather_second(acts, 1)
    swap_enc.wait_recv()
    split_weights(1)
    wait_all(own_rest)

    def encode(chunk):
        at = pl.ds(chunk * CHUNK, CHUNK)
        part[0, at] = product(acts[at], wenc_h[...], wenc_l[...], plain)
        sum_start(0, chunk)

    encode(0)
    other_rest = gather_forward(acts, 1, other_second)
    encode(1)
    sum_middle(0, 0)
    sum_middle(0, 1)
    wait_all(other_rest)
    encode(2)
    encode(3)
    give_acts = send(acts, acts_sib, sibling)
    split_decoder(0)
    swap_dec.wait_recv()
    split_decoder(1)
    sum_middle(0, 2)
    sum_middle(0, 3)

    bias_row = bias
    bias_row[:, 0:256] = benc_ref[0:1, :]
    swap_bias = send(bias.at[:, pl.ds(0, 256)], bias.at[:, pl.ds(256, 256)], sibling)
    swap_bias.wait_recv()

    def decode(chunk):
        at = pl.ds(chunk * CHUNK, CHUNK)
        sum_finish(0, chunk)
        codes, gate = softplus_and_sigmoid(sig[at] + bias[...])
        sig[at] = gate
        high, low = split(codes)
        both = jnp.concatenate([high, low], axis=0)
        for block in range(3):
            cols = slice(block * 768, (block + 1) * 768)
            main = jnp.dot(both, wdec_h[:, cols], preferred_element_type=F32)
            cross = jnp.dot(high, wdec_l[:, cols], preferred_element_type=F32)
            recon[at, cols] = main[:CHUNK] + (main[CHUNK:] + cross)

    half = 2 * UNIT

    def scatter_start(plane):
        base = row(plane, 3, 0)
        a = send(rows(recon, base, half), far_a.at[plane], second(1))
        b = send(rows(recon, base + half, half), far_b.at[plane], second(-1))
        up1 = send(rows(recon, row(plane, 1, 0) + half, half), from_down.at[plane, pl.ds(half, half)], second(1))
        down0 = send(rows(recon, row(plane, 2, 0), half), from_up.at[plane, pl.ds(0, half)], second(-1))
        return a, b, up1, down0

    def scatter_add(plane, copies):
        a, b, up1, down0 = copies
        to_up = pl.ds(row(plane, 1, 0), half)
        to_down = pl.ds(row(plane, 2, 0) + half, half)
        a.wait_recv()
        recon[to_up] = recon[to_up] + far_a[plane]
        up0 = send(recon.at[to_up], from_down.at[plane, pl.ds(0, half)], second(1))
        b.wait_recv()
        recon[to_down] = recon[to_down] + far_b[plane]
        down1 = send(recon.at[to_down], from_up.at[plane, pl.ds(half, half)], second(-1))
        return up1, down0, up0, down1

    def scatter_first(plane, copies):
        wait_all(copies)
        row_sum[plane] = recon[pl.ds(row(plane, 0, 0), 4 * UNIT)] + (from_up[plane] + from_down[plane])
        return [
            send(row_sum.at[plane, pl.ds(UNIT, UNIT)], first_in.at[plane, 0], first(1)),
            send(row_sum.at[plane, pl.ds(2 * UNIT, UNIT)], first_in.at[plane, 1], first(-1)),
            send(row_sum.at[plane, pl.ds(3 * UNIT, UNIT)], first_in.at[plane, 2], first(2)),
        ]

    def scatter_total(plane, copies):
        wait_all(copies)
        return row_sum[plane, 0:UNIT] + (first_in[plane, 0] + (first_in[plane, 1] + first_in[plane, 2]))

    decode(0)
    decode(1)
    own_scatter = scatter_start(0)
    decode(2)
    own_scatter = scatter_add(0, own_scatter)
    decode(3)
    other_scatter = scatter_start(1)
    own_scatter = scatter_first(0, own_scatter)
    other_scatter = scatter_add(1, other_scatter)
    other_scatter = scatter_first(1, other_scatter)
    own_total = scatter_total(0, own_scatter)
    plane_out[...] = scatter_total(1, other_scatter)
    to_home = send(plane_out, plane_in, other_plane)
    to_home.wait_recv()
    resid[0:UNIT, :] = (own_total + plane_in[...]) + bdec_ref[...] - acts[0:UNIT, :]

    to_plane, own_first = start_gather(resid)
    wait_all(own_first)
    own_second = gather_second(resid, 0)
    to_plane.wait_recv()
    other_first = gather_first(resid, 1)
    own_rest = gather_forward(resid, 0, own_second)
    wait_all(other_first)
    other_second = gather_second(resid, 1)
    wait_all(own_rest)

    def code_gradient(chunk):
        at = pl.ds(chunk * CHUNK, CHUNK)
        part[1, at] = product(resid[at], wdec_h[...], wdec_l[...], turned) + norms[0:1, :]
        sum_start(1, chunk)

    pre_sig = pg
    pre_sig[...] = sig[...]
    code_gradient(0)
    other_rest = gather_forward(resid, 1, other_second)
    code_gradient(1)
    sum_middle(1, 0)
    sum_middle(1, 1)
    wait_all(other_rest)
    code_gradient(2)
    code_gradient(3)

    give_acts.wait_recv()

    def turn(i, _):
        cols = pl.ds(pl.multiple_of(i * 256, 256), 256)
        for half_at, ref in ((0, acts), (256, acts_sib)):
            high, low = split(jnp.transpose(ref[:, cols]))
            acts_th[cols, half_at : half_at + 256] = high
            acts_tl[cols, half_at : half_at + 256] = low
        return 0

    lax.fori_loop(0, 9, turn, 0)

    sum_middle(1, 2)
    sum_middle(1, 3)
    gives = []
    for chunk in chunks:
        at = pl.ds(chunk * CHUNK, CHUNK)
        sum_finish(1, chunk)
        pg[at] = pg[at] * sig[at]
        gives.append(send(pg.at[at, pl.ds(256, 256)], pg_in.at[at], sibling))
    wait_all(gives)

    mine = pg[:, 0:256]
    theirs = pg_in[...]
    gbias_ref[...] = jnp.sum(mine, axis=0, keepdims=True) + jnp.sum(theirs, axis=0, keepdims=True)
    right_h, right_l = split(jnp.concatenate([mine, theirs], axis=0))

    stores = []
    for i in range(9):
        at = pl.ds(i * 256, 256)
        high = acts_th[at, :]
        main = jnp.dot(high, right_h, preferred_element_type=F32)
        cross = jnp.dot(high, right_l, preferred_element_type=F32) + jnp.dot(
            acts_tl[at, :], right_h, preferred_element_type=F32
        )
        grad_buf[at, :] = main + cross
        store = pltpu.make_async_copy(grad_buf.at[at], grad_hbm.at[0, at], lsem.at[3 + i])
        store.start()
        stores.append(store)

    for copy in sent:
        copy.wait_send()
    for phase in range(2):
        for chunk in chunks:
            sum_drain(phase, chunk)
    for store in stores:
        store.wait()


def on_device(acts, w_enc, b_enc, w_dec, b_dec):
    depth = acts.shape[2]
    w_dec = w_dec.reshape(256, depth)
    any_space = pl.BlockSpec(memory_space=pl.ANY)
    vmem = pl.BlockSpec(memory_space=pltpu.VMEM)
    copies = 110
    grad, bias = pl.pallas_call(
        kernel,
        out_shape=(
            jax.ShapeDtypeStruct((1, depth, 256), F32),
            jax.ShapeDtypeStruct((1, 256), F32),
        ),
        in_specs=[any_space, any_space, any_space, vmem, vmem],
        out_specs=(any_space, vmem),
        scratch_shapes=[
            pltpu.VMEM((256, depth), F32),
            pltpu.VMEM((256, depth), F32),
            pltpu.VMEM((256, depth), F32),
            pltpu.VMEM((2, depth, 256), F32),
            pltpu.VMEM((2, 256, depth), F32),
            pltpu.VMEM((depth, 512), BF16),
            pltpu.VMEM((depth, 512), BF16),
            pltpu.VMEM((512, depth), BF16),
            pltpu.VMEM((512, depth), BF16),
            pltpu.VMEM((1, 512), F32),
            pltpu.VMEM((8, 512), F32),
            pltpu.VMEM((256, depth), F32),
            pltpu.VMEM((2, 32, depth), F32),
            pltpu.VMEM((2, 16, depth), F32),
            pltpu.VMEM((2, 16, depth), F32),
            pltpu.VMEM((2, 32, depth), F32),
            pltpu.VMEM((2, 32, depth), F32),
            pltpu.VMEM((2, 3, 8, depth), F32),
            pltpu.VMEM((8, depth), F32),
            pltpu.VMEM((8, depth), F32),
            pltpu.VMEM((2, 256, 512), F32),
            pltpu.VMEM((2, 256, 512), F32),
            pltpu.VMEM((2, 256, 512), F32),
            pltpu.VMEM((2, 256, 512), F32),
            pltpu.VMEM((2, 256, 512), F32),
            pltpu.VMEM((256, 512), F32),
            pltpu.VMEM((256, 512), F32),
            pltpu.VMEM((256, 256), F32),
            pltpu.VMEM((depth, 512), BF16),
            pltpu.VMEM((depth, 512), BF16),
            pltpu.VMEM((depth, 256), F32),
            pltpu.SemaphoreType.DMA((copies,)),
            pltpu.SemaphoreType.DMA((copies,)),
            pltpu.SemaphoreType.DMA((12,)),
        ],
        compiler_params=pltpu.CompilerParams(
            collective_id=0, has_side_effects=True, vmem_limit_bytes=60 * 1024 * 1024
        ),
        cost_estimate=pl.CostEstimate(flops=7_300_000_000, bytes_accessed=10_000_000, transcendentals=500_000),
        name="crosscoder_gradient",
    )(acts, w_enc, w_dec, b_dec, b_enc.reshape(1, 256))
    return grad, bias.reshape(256)


def solution(mesh):
    return jax.shard_map(
        on_device,
        mesh=mesh,
        in_specs=(
            P("layer", "latent", None),
            P("layer", None, "latent"),
            P("latent"),
            P("latent", "layer", None),
            P("layer", None),
        ),
        out_specs=(P("layer", None, "latent"), P("latent")),
        check_vma=False,
    )
```

```python
import functools

import jax
import jax.numpy as jnp
from jax import lax
from jax.experimental import pallas as pl
from jax.experimental.pallas import tpu as pltpu
from jax.sharding import PartitionSpec as P

SHARP = 4.0
MESH = pl.DeviceIdType.MESH
F32 = jnp.float32
BF16 = jnp.bfloat16

STEPS = (0, 1, -1, 2)
UNIT = 8
CHUNK = 64


def split(value):
    high = value.astype(BF16)
    return high, (value - high.astype(F32)).astype(BF16)


def softplus_and_sigmoid(pre):
    x = SHARP * pre
    e = jnp.exp(-jnp.abs(x))
    codes = (jnp.maximum(x, 0.0) + jnp.log1p(e)) / SHARP
    inv = 1.0 / (1.0 + e)
    return codes, jnp.where(x >= 0, inv, e * inv)


def kernel(
    acts_hbm,
    wenc_hbm,
    wdec_hbm,
    bdec_ref,
    benc_ref,
    grad_hbm,
    gbias_ref,
    acts,
    acts_sib,
    resid,
    wenc,
    wdec,
    wenc_h,
    wenc_l,
    wdec_h,
    wdec_l,
    bias,
    norms,
    recon,
    row_sum,
    far_a,
    far_b,
    from_up,
    from_down,
    first_in,
    plane_out,
    plane_in,
    part,
    near_in,
    inner_out,
    far_in,
    outer_out,
    sig,
    pg,
    pg_in,
    acts_th,
    acts_tl,
    grad_buf,
    ssem,
    rsem,
    lsem,
):
    layer = lax.axis_index("layer")
    place = lax.axis_index("latent")
    core = lax.rem(place, 2)
    x = lax.rem(place // 2, 4)
    z_hi = lax.rem(place // 8, 2)
    y = place // 16

    def device(dx, dy, dz, dc):
        nx = lax.rem(x + dx + 4, 4)
        ny = lax.rem(y + dy + 4, 4)
        nz = lax.rem(z_hi + dz, 2)
        nc = lax.rem(core + dc, 2)
        return (layer, ((ny * 2 + nz) * 4 + nx) * 2 + nc)

    def first(d):
        return device(d * (1 - core), d * core, 0, 0)

    def second(d):
        return device(d * core, d * (1 - core), 0, 0)

    other_plane = device(0, 0, 1, 0)
    sibling = device(0, 0, 0, 1)
    upper = layer // 2
    inner = lax.rem(layer + upper, 2)
    toward = 1 - 2 * upper
    far = (layer + toward, place)
    near = (layer - toward, place)

    state = {"next": 0}
    sent = []

    def copy_to(src, dst, target, index=None):
        if index is None:
            index = state["next"]
            state["next"] += 1
        return pltpu.make_async_remote_copy(
            src_ref=src,
            dst_ref=dst,
            send_sem=ssem.at[index],
            recv_sem=rsem.at[index],
            device_id=target,
            device_id_type=MESH,
        )

    def send(src, dst, target):
        copy = copy_to(src, dst, target)
        copy.start()
        sent.append(copy)
        return copy

    load_acts = pltpu.make_async_copy(acts_hbm.at[0], acts.at[pl.ds(0, UNIT)], lsem.at[0])
    load_enc = pltpu.make_async_copy(wenc_hbm.at[0], wenc.at[0], lsem.at[1])
    load_dec = pltpu.make_async_copy(wdec_hbm.at[:, 0], wdec.at[0], lsem.at[2])
    load_acts.start()
    load_enc.start()
    load_dec.start()

    barrier = pltpu.get_barrier_semaphore()
    partners = [first(1), first(-1), first(2), second(1), second(-1), other_plane, sibling, far]
    for partner in partners:
        pl.semaphore_signal(barrier, inc=1, device_id=partner, device_id_type=MESH)

    @pl.when(inner == 1)
    def _():
        pl.semaphore_signal(barrier, inc=1, device_id=near, device_id_type=MESH)

    pl.semaphore_wait(barrier, len(partners) + inner)

    def row(plane, b, a):
        return ((plane * 4 + b) * 4 + a) * UNIT

    def rows(ref, start, count):
        return ref.at[pl.ds(start, count)]

    def gather_first(ref, plane):
        own = rows(ref, row(plane, 0, 0), UNIT)
        return [
            send(own, rows(ref, row(plane, 0, 2), UNIT), first(1)),
            send(own, rows(ref, row(plane, 0, 1), UNIT), first(-1)),
            send(own, rows(ref, row(plane, 0, 3), UNIT), first(2)),
        ]

    def gather_second(ref, plane):
        half = 2 * UNIT
        own = row(plane, 0, 0)
        up = row(plane, 2, 0)
        down = row(plane, 1, 0)
        up0 = send(rows(ref, own, half), rows(ref, up, half), second(1))
        down1 = send(rows(ref, own + half, half), rows(ref, down + half, half), second(-1))
        up1 = send(rows(ref, own + half, half), rows(ref, up + half, half), second(1))
        down0 = send(rows(ref, own, half), rows(ref, down, half), second(-1))
        return up0, down1, up1, down0

    def gather_forward(ref, plane, copies):
        half = 2 * UNIT
        up0, down1, up1, down0 = copies
        last = row(plane, 3, 0)
        up0.wait_recv()
        fwd0 = send(rows(ref, row(plane, 2, 0), half), rows(ref, last, half), second(1))
        down1.wait_recv()
        fwd1 = send(rows(ref, row(plane, 1, 0) + half, half), rows(ref, last + half, half), second(-1))
        return up1, down0, fwd0, fwd1

    def wait_all(copies):
        for copy in copies:
            copy.wait_recv()

    def start_gather(ref):
        to_plane = send(rows(ref, 0, UNIT), rows(ref, row(1, 0, 0), UNIT), other_plane)
        return to_plane, gather_first(ref, 0)

    def split_weights(slot):
        def enc(i, _):
            at = pl.ds(pl.multiple_of(i * 256, 256), 256)
            high, low = split(wenc[slot, at, :])
            wenc_h[at, slot * 256 : (slot + 1) * 256] = high
            wenc_l[at, slot * 256 : (slot + 1) * 256] = low
            return 0

        lax.fori_loop(0, 9, enc, 0)

    def split_decoder(slot):
        def dec(i, _):
            at = pl.ds(pl.multiple_of(i * 32, 32), 32)
            to = pl.ds(pl.multiple_of(slot * 256 + i * 32, 32), 32)
            high, low = split(wdec[slot, at, :])
            wdec_h[to, :] = high
            wdec_l[to, :] = low
            return 0

        lax.fori_loop(0, 8, dec, 0)
        square = wdec[slot] * wdec[slot]
        total = lax.dot_general(
            jnp.ones((8, square.shape[1]), F32),
            square,
            (((1,), (1,)), ((), ())),
            precision=lax.Precision.HIGHEST,
            preferred_element_type=F32,
        )
        norms[:, slot * 256 : (slot + 1) * 256] = jnp.sqrt(total)

    def product(left, right_h, right_l, dims):
        high, low = split(left)
        count = left.shape[0]
        both = lax.dot_general(jnp.concatenate([high, low], axis=0), right_h, dims, preferred_element_type=F32)
        cross = lax.dot_general(high, right_l, dims, preferred_element_type=F32)
        return both[:count] + (both[count:] + cross)

    def sum_index(phase, chunk):
        return state["sum"] + phase * 3 * (256 // CHUNK) + chunk * 3

    def sum_start(phase, chunk):
        at = pl.ds(chunk * CHUNK, CHUNK)
        index = sum_index(phase, chunk)

        @pl.when(inner == 0)
        def _():
            copy_to(part.at[phase, at], near_in.at[phase, at], far, index).start()

    def sum_middle(phase, chunk):
        at = pl.ds(chunk * CHUNK, CHUNK)
        index = sum_index(phase, chunk)

        @pl.when(inner == 1)
        def _():
            copy_to(part.at[phase, at], near_in.at[phase, at], far, index).wait_recv()
            inner_out[phase, at] = part[phase, at] + near_in[phase, at]
            copy_to(inner_out.at[phase, at], far_in.at[phase, at], far, index + 1).start()

    def sum_finish(phase, chunk):
        at = pl.ds(chunk * CHUNK, CHUNK)
        index = sum_index(phase, chunk)
        copy_to(inner_out.at[phase, at], far_in.at[phase, at], far, index + 1).wait_recv()

        @pl.when(inner == 1)
        def _():
            outer_out[phase, at] = part[phase, at] + far_in[phase, at]
            pltpu.make_async_remote_copy(
                src_ref=outer_out.at[phase, at],
                dst_ref=far_in.at[phase, at],
                send_sem=ssem.at[index + 2],
                recv_sem=rsem.at[index + 1],
                device_id=near,
                device_id_type=MESH,
            ).start()
            inner_out_value = inner_out[phase, at]
            sig[at] = inner_out_value + far_in[phase, at]

        @pl.when(inner == 0)
        def _():
            sig[at] = part[phase, at] + far_in[phase, at]

    def sum_drain(phase, chunk):
        at = pl.ds(chunk * CHUNK, CHUNK)
        index = sum_index(phase, chunk)

        @pl.when(inner == 0)
        def _():
            copy_to(part.at[phase, at], near_in.at[phase, at], far, index).wait_send()

        @pl.when(inner == 1)
        def _():
            copy_to(inner_out.at[phase, at], far_in.at[phase, at], far, index + 1).wait_send()
            copy_to(outer_out.at[phase, at], far_in.at[phase, at], near, index + 2).wait_send()

    state["sum"] = 0
    state["next"] = 2 * 3 * (256 // CHUNK)
    chunks = range(256 // CHUNK)
    plain = (((1,), (0,)), ((), ()))
    turned = (((1,), (1,)), ((), ()))

    load_acts.wait()
    to_plane, own_first = start_gather(acts)
    load_enc.wait()
    swap_enc = send(wenc.at[0], wenc.at[1], sibling)
    load_dec.wait()
    swap_dec = send(wdec.at[0], wdec.at[1], sibling)
    bias[:, 0:256] = benc_ref[0:1, :]
    swap_bias = send(bias.at[:, pl.ds(0, 256)], bias.at[:, pl.ds(256, 256)], sibling)
    wait_all(own_first)
    own_second = gather_second(acts, 0)
    split_weights(0)
    to_plane.wait_recv()
    other_first = gather_first(acts, 1)
    own_rest = gather_forward(acts, 0, own_second)
    swap_enc.wait_recv()
    split_weights(1)
    wait_all(other_first)
    other_second = gather_second(acts, 1)
    wait_all(own_rest)

    def encode(chunk):
        at = pl.ds(chunk * CHUNK, CHUNK)
        part[0, at] = product(acts[at], wenc_h[...], wenc_l[...], plain)
        sum_start(0, chunk)

    encode(0)
    encode(1)
    split_decoder(0)
    other_rest = gather_forward(acts, 1, other_second)
    sum_middle(0, 0)
    sum_middle(0, 1)
    swap_dec.wait_recv()
    split_decoder(1)
    wait_all(other_rest)
    encode(2)
    encode(3)
    give_acts = send(acts, acts_sib, sibling)
    swap_bias.wait_recv()
    sum_middle(0, 2)
    sum_middle(0, 3)

    def decode(chunk):
        at = pl.ds(chunk * CHUNK, CHUNK)
        sum_finish(0, chunk)
        codes, gate = softplus_and_sigmoid(sig[at] + bias[...])
        sig[at] = gate
        high, low = split(codes)
        both = jnp.concatenate([high, low], axis=0)
        for block in range(3):
            cols = slice(block * 768, (block + 1) * 768)
            main = jnp.dot(both, wdec_h[:, cols], preferred_element_type=F32)
            cross = jnp.dot(high, wdec_l[:, cols], preferred_element_type=F32)
            recon[at, cols] = main[:CHUNK] + (main[CHUNK:] + cross)

    half = 2 * UNIT

    def scatter_start(plane):
        base = row(plane, 3, 0)
        a = send(rows(recon, base, half), far_a.at[plane], second(1))
        b = send(rows(recon, base + half, half), far_b.at[plane], second(-1))
        up1 = send(rows(recon, row(plane, 1, 0) + half, half), from_down.at[plane, pl.ds(half, half)], second(1))
        down0 = send(rows(recon, row(plane, 2, 0), half), from_up.at[plane, pl.ds(0, half)], second(-1))
        return a, b, up1, down0

    def scatter_add(plane, copies):
        a, b, up1, down0 = copies
        to_up = pl.ds(row(plane, 1, 0), half)
        to_down = pl.ds(row(plane, 2, 0) + half, half)
        a.wait_recv()
        recon[to_up] = recon[to_up] + far_a[plane]
        up0 = send(recon.at[to_up], from_down.at[plane, pl.ds(0, half)], second(1))
        b.wait_recv()
        recon[to_down] = recon[to_down] + far_b[plane]
        down1 = send(recon.at[to_down], from_up.at[plane, pl.ds(half, half)], second(-1))
        return up1, down0, up0, down1

    def scatter_first(plane, copies):
        wait_all(copies)
        row_sum[plane] = recon[pl.ds(row(plane, 0, 0), 4 * UNIT)] + (from_up[plane] + from_down[plane])
        return [
            send(row_sum.at[plane, pl.ds(UNIT, UNIT)], first_in.at[plane, 0], first(1)),
            send(row_sum.at[plane, pl.ds(2 * UNIT, UNIT)], first_in.at[plane, 1], first(-1)),
            send(row_sum.at[plane, pl.ds(3 * UNIT, UNIT)], first_in.at[plane, 2], first(2)),
        ]

    def scatter_total(plane, copies):
        wait_all(copies)
        return row_sum[plane, 0:UNIT] + (first_in[plane, 0] + (first_in[plane, 1] + first_in[plane, 2]))

    decode(0)
    decode(1)
    own_scatter = scatter_start(0)
    decode(2)
    own_scatter = scatter_add(0, own_scatter)
    decode(3)
    other_scatter = scatter_start(1)
    own_scatter = scatter_first(0, own_scatter)
    other_scatter = scatter_add(1, other_scatter)
    other_scatter = scatter_first(1, other_scatter)
    plane_out[0] = scatter_total(0, own_scatter)
    own_to_plane = send(plane_out.at[0], plane_in.at[0], other_plane)
    other_total = scatter_total(1, other_scatter)
    plane_out[1] = other_total
    other_to_plane = send(plane_out.at[1], plane_in.at[1], other_plane)

    def residual(plane, total):
        at = pl.ds(row(plane, 0, 0), UNIT)
        resid[at] = total + bdec_ref[...] - acts[at]

    def turn(i, _):
        cols = pl.ds(pl.multiple_of(i * 256, 256), 256)
        for half_at, ref in ((0, acts), (256, acts_sib)):
            high, low = split(jnp.transpose(ref[:, cols]))
            acts_th[cols, half_at : half_at + 256] = high
            acts_tl[cols, half_at : half_at + 256] = low
        return 0

    own_to_plane.wait_recv()
    residual(1, other_total + plane_in[0])
    other_first = gather_first(resid, 1)
    give_acts.wait_recv()
    lax.fori_loop(0, 4, turn, 0)
    wait_all(other_first)
    other_second = gather_second(resid, 1)
    lax.fori_loop(4, 6, turn, 0)
    other_to_plane.wait_recv()
    residual(0, plane_out[0] + plane_in[1])
    own_first = gather_first(resid, 0)
    other_rest = gather_forward(resid, 1, other_second)
    lax.fori_loop(6, 9, turn, 0)
    wait_all(own_first)
    own_second = gather_second(resid, 0)
    wait_all(other_rest)

    def code_gradient(chunk):
        at = pl.ds(chunk * CHUNK, CHUNK)
        part[1, at] = product(resid[at], wdec_h[...], wdec_l[...], turned) + norms[0:1, :]
        sum_start(1, chunk)

    pre_sig = pg
    pre_sig[...] = sig[...]
    code_gradient(2)
    code_gradient(3)
    own_rest = gather_forward(resid, 0, own_second)
    sum_middle(1, 2)
    sum_middle(1, 3)
    wait_all(own_rest)
    code_gradient(0)
    code_gradient(1)
    sum_middle(1, 0)
    sum_middle(1, 1)
    gives = []
    for chunk in (2, 3, 0, 1):
        at = pl.ds(chunk * CHUNK, CHUNK)
        sum_finish(1, chunk)
        pg[at] = pg[at] * sig[at]
        gives.append(send(pg.at[at, pl.ds(256, 256)], pg_in.at[at], sibling))
    wait_all(gives)

    mine = pg[:, 0:256]
    theirs = pg_in[...]
    gbias_ref[...] = jnp.sum(mine, axis=0, keepdims=True) + jnp.sum(theirs, axis=0, keepdims=True)
    right_h, right_l = split(jnp.concatenate([mine, theirs], axis=0))

    stores = []
    for i in range(9):
        at = pl.ds(i * 256, 256)
        high = acts_th[at, :]
        main = jnp.dot(high, right_h, preferred_element_type=F32)
        cross = jnp.dot(high, right_l, preferred_element_type=F32) + jnp.dot(
            acts_tl[at, :], right_h, preferred_element_type=F32
        )
        grad_buf[at, :] = main + cross
        store = pltpu.make_async_copy(grad_buf.at[at], grad_hbm.at[0, at], lsem.at[3 + i])
        store.start()
        stores.append(store)

    for copy in sent:
        copy.wait_send()
    for phase in range(2):
        for chunk in chunks:
            sum_drain(phase, chunk)
    for store in stores:
        store.wait()


def on_device(acts, w_enc, b_enc, w_dec, b_dec):
    depth = acts.shape[2]
    any_space = pl.BlockSpec(memory_space=pl.ANY)
    vmem = pl.BlockSpec(memory_space=pltpu.VMEM)
    copies = 110
    grad, bias = pl.pallas_call(
        kernel,
        out_shape=(
            jax.ShapeDtypeStruct((1, depth, 256), F32),
            jax.ShapeDtypeStruct((1, 256), F32),
        ),
        in_specs=[any_space, any_space, any_space, vmem, vmem],
        out_specs=(any_space, vmem),
        scratch_shapes=[
            pltpu.VMEM((256, depth), F32),
            pltpu.VMEM((256, depth), F32),
            pltpu.VMEM((256, depth), F32),
            pltpu.VMEM((2, depth, 256), F32),
            pltpu.VMEM((2, 256, depth), F32),
            pltpu.VMEM((depth, 512), BF16),
            pltpu.VMEM((depth, 512), BF16),
            pltpu.VMEM((512, depth), BF16),
            pltpu.VMEM((512, depth), BF16),
            pltpu.VMEM((1, 512), F32),
            pltpu.VMEM((8, 512), F32),
            pltpu.VMEM((256, depth), F32),
            pltpu.VMEM((2, 32, depth), F32),
            pltpu.VMEM((2, 16, depth), F32),
            pltpu.VMEM((2, 16, depth), F32),
            pltpu.VMEM((2, 32, depth), F32),
            pltpu.VMEM((2, 32, depth), F32),
            pltpu.VMEM((2, 3, 8, depth), F32),
            pltpu.VMEM((2, 8, depth), F32),
            pltpu.VMEM((2, 8, depth), F32),
            pltpu.VMEM((2, 256, 512), F32),
            pltpu.VMEM((2, 256, 512), F32),
            pltpu.VMEM((2, 256, 512), F32),
            pltpu.VMEM((2, 256, 512), F32),
            pltpu.VMEM((2, 256, 512), F32),
            pltpu.VMEM((256, 512), F32),
            pltpu.VMEM((256, 512), F32),
            pltpu.VMEM((256, 256), F32),
            pltpu.VMEM((depth, 512), BF16),
            pltpu.VMEM((depth, 512), BF16),
            pltpu.VMEM((depth, 256), F32),
            pltpu.SemaphoreType.DMA((copies,)),
            pltpu.SemaphoreType.DMA((copies,)),
            pltpu.SemaphoreType.DMA((12,)),
        ],
        compiler_params=pltpu.CompilerParams(
            collective_id=0, has_side_effects=True, vmem_limit_bytes=60 * 1024 * 1024
        ),
        cost_estimate=pl.CostEstimate(flops=7_300_000_000, bytes_accessed=10_000_000, transcendentals=500_000),
        name="crosscoder_gradient",
    )(acts, w_enc, w_dec, b_dec, b_enc.reshape(1, 256))
    return grad, bias.reshape(256)


def solution(mesh):
    return jax.shard_map(
        on_device,
        mesh=mesh,
        in_specs=(
            P("layer", "latent", None),
            P("layer", None, "latent"),
            P("latent"),
            P("latent", "layer", None),
            P("layer", None),
        ),
        out_specs=(P("layer", None, "latent"), P("latent")),
        check_vma=False,
    )
```

```python
import functools

import jax
import jax.numpy as jnp
from jax import lax
from jax.experimental import pallas as pl
from jax.experimental.pallas import tpu as pltpu
from jax.sharding import PartitionSpec as P

SHARP = 4.0
MESH = pl.DeviceIdType.MESH
F32 = jnp.float32
BF16 = jnp.bfloat16

STEPS = (0, 1, -1, 2)
UNIT = 8
CHUNKS = ((0, 32), (32, 64), (96, 32), (128, 32), (160, 64), (224, 32))


def split(value):
    high = value.astype(BF16)
    return high, (value - high.astype(F32)).astype(BF16)


def softplus_and_sigmoid(pre):
    x = SHARP * pre
    e = jnp.exp(-jnp.abs(x))
    codes = (jnp.maximum(x, 0.0) + jnp.log1p(e)) / SHARP
    inv = 1.0 / (1.0 + e)
    return codes, jnp.where(x >= 0, inv, e * inv)


def kernel(
    acts_hbm,
    wenc_hbm,
    wdec_hbm,
    bdec_ref,
    benc_ref,
    grad_hbm,
    gbias_ref,
    acts,
    acts_sib,
    resid,
    wenc,
    wdec,
    wenc_h,
    wenc_l,
    wdec_h,
    wdec_l,
    bias,
    norms,
    recon,
    row_sum,
    far_a,
    far_b,
    from_up,
    from_down,
    first_in,
    plane_out,
    plane_in,
    part,
    near_in,
    inner_out,
    far_in,
    outer_out,
    sig,
    pg,
    pg_in,
    acts_th,
    acts_tl,
    grad_buf,
    ssem,
    rsem,
    lsem,
):
    layer = lax.axis_index("layer")
    place = lax.axis_index("latent")
    core = lax.rem(place, 2)
    x = lax.rem(place // 2, 4)
    z_hi = lax.rem(place // 8, 2)
    y = place // 16

    def device(dx, dy, dz, dc):
        nx = lax.rem(x + dx + 4, 4)
        ny = lax.rem(y + dy + 4, 4)
        nz = lax.rem(z_hi + dz, 2)
        nc = lax.rem(core + dc, 2)
        return (layer, ((ny * 2 + nz) * 4 + nx) * 2 + nc)

    def first(d):
        return device(d * (1 - core), d * core, 0, 0)

    def second(d):
        return device(d * core, d * (1 - core), 0, 0)

    other_plane = device(0, 0, 1, 0)
    sibling = device(0, 0, 0, 1)
    upper = layer // 2
    inner = lax.rem(layer + upper, 2)
    toward = 1 - 2 * upper
    far = (layer + toward, place)
    near = (layer - toward, place)

    state = {"next": 0}
    sent = []

    def copy_to(src, dst, target, index=None):
        if index is None:
            index = state["next"]
            state["next"] += 1
        return pltpu.make_async_remote_copy(
            src_ref=src,
            dst_ref=dst,
            send_sem=ssem.at[index],
            recv_sem=rsem.at[index],
            device_id=target,
            device_id_type=MESH,
        )

    def send(src, dst, target):
        copy = copy_to(src, dst, target)
        copy.start()
        sent.append(copy)
        return copy

    load_acts = pltpu.make_async_copy(acts_hbm.at[0], acts.at[pl.ds(0, UNIT)], lsem.at[0])
    load_enc = pltpu.make_async_copy(wenc_hbm.at[0], wenc.at[0], lsem.at[1])
    load_dec = pltpu.make_async_copy(wdec_hbm.at[:, 0], wdec.at[0], lsem.at[2])
    load_acts.start()
    load_enc.start()
    load_dec.start()

    barrier = pltpu.get_barrier_semaphore()
    partners = [first(1), first(-1), first(2), second(1), second(-1), other_plane, sibling, far]
    for partner in partners:
        pl.semaphore_signal(barrier, inc=1, device_id=partner, device_id_type=MESH)

    @pl.when(inner == 1)
    def _():
        pl.semaphore_signal(barrier, inc=1, device_id=near, device_id_type=MESH)

    pl.semaphore_wait(barrier, len(partners) + inner)

    def row(plane, b, a):
        return ((plane * 4 + b) * 4 + a) * UNIT

    def rows(ref, start, count):
        return ref.at[pl.ds(start, count)]

    def gather_first(ref, plane):
        own = rows(ref, row(plane, 0, 0), UNIT)
        return [
            send(own, rows(ref, row(plane, 0, 2), UNIT), first(1)),
            send(own, rows(ref, row(plane, 0, 1), UNIT), first(-1)),
            send(own, rows(ref, row(plane, 0, 3), UNIT), first(2)),
        ]

    def gather_second(ref, plane):
        half = 2 * UNIT
        own = row(plane, 0, 0)
        up = row(plane, 2, 0)
        down = row(plane, 1, 0)
        up0 = send(rows(ref, own, half), rows(ref, up, half), second(1))
        down1 = send(rows(ref, own + half, half), rows(ref, down + half, half), second(-1))
        up1 = send(rows(ref, own + half, half), rows(ref, up + half, half), second(1))
        down0 = send(rows(ref, own, half), rows(ref, down, half), second(-1))
        return up0, down1, up1, down0

    def gather_forward(ref, plane, copies):
        half = 2 * UNIT
        up0, down1, up1, down0 = copies
        last = row(plane, 3, 0)
        up0.wait_recv()
        fwd0 = send(rows(ref, row(plane, 2, 0), half), rows(ref, last, half), second(1))
        down1.wait_recv()
        fwd1 = send(rows(ref, row(plane, 1, 0) + half, half), rows(ref, last + half, half), second(-1))
        return up1, down0, fwd0, fwd1

    def wait_all(copies):
        for copy in copies:
            copy.wait_recv()

    def start_gather(ref):
        to_plane = send(rows(ref, 0, UNIT), rows(ref, row(1, 0, 0), UNIT), other_plane)
        return to_plane, gather_first(ref, 0)

    def split_weights(slot):
        def enc(i, _):
            at = pl.ds(pl.multiple_of(i * 256, 256), 256)
            high, low = split(wenc[slot, at, :])
            wenc_h[at, slot * 256 : (slot + 1) * 256] = high
            wenc_l[at, slot * 256 : (slot + 1) * 256] = low
            return 0

        lax.fori_loop(0, 9, enc, 0)

    def split_decoder(slot):
        def dec(i, _):
            at = pl.ds(pl.multiple_of(i * 32, 32), 32)
            to = pl.ds(pl.multiple_of(slot * 256 + i * 32, 32), 32)
            high, low = split(wdec[slot, at, :])
            wdec_h[to, :] = high
            wdec_l[to, :] = low
            return 0

        lax.fori_loop(0, 8, dec, 0)
        squares = jnp.zeros((256, 128), F32)
        for k in range(wdec.shape[2] // 128):
            value = wdec[slot, :, k * 128 : (k + 1) * 128]
            squares = squares + value * value
        total = lax.dot_general(
            jnp.ones((8, 128), F32),
            squares,
            (((1,), (1,)), ((), ())),
            precision=lax.Precision.HIGHEST,
            preferred_element_type=F32,
        )
        norms[:, slot * 256 : (slot + 1) * 256] = jnp.sqrt(total)

    def product(left, right_h, right_l, dims):
        high, low = split(left)
        count = left.shape[0]
        both = lax.dot_general(jnp.concatenate([high, low], axis=0), right_h, dims, preferred_element_type=F32)
        cross = lax.dot_general(high, right_l, dims, preferred_element_type=F32)
        return both[:count] + (both[count:] + cross)

    def sum_place(phase, chunk):
        start, count = CHUNKS[chunk]
        return pl.ds(start, count), (phase * len(CHUNKS) + chunk) * 3

    def sum_in(phase, chunk):
        at, index = sum_place(phase, chunk)
        return copy_to(part.at[phase, at], near_in.at[phase, at], far, index)

    def sum_swap(phase, chunk):
        at, index = sum_place(phase, chunk)
        return copy_to(inner_out.at[phase, at], far_in.at[phase, at], far, index + 1)

    def sum_out(phase, chunk):
        at, index = sum_place(phase, chunk)
        return pltpu.make_async_remote_copy(
            src_ref=outer_out.at[phase, at],
            dst_ref=far_in.at[phase, at],
            send_sem=ssem.at[index + 2],
            recv_sem=rsem.at[index + 1],
            device_id=near,
            device_id_type=MESH,
        )

    def sum_start(phase, chunk):
        @pl.when(inner == 0)
        def _():
            sum_in(phase, chunk).start()

    def sum_middle(phase, chunk):
        at, _ = sum_place(phase, chunk)

        @pl.when(inner == 1)
        def _():
            sum_in(phase, chunk).wait_recv()
            inner_out[phase, at] = part[phase, at] + near_in[phase, at]
            sum_swap(phase, chunk).start()

    def sum_relay(phase, chunk):
        at, _ = sum_place(phase, chunk)

        @pl.when(inner == 1)
        def _():
            sum_swap(phase, chunk).wait_recv()
            outer_out[phase, at] = part[phase, at] + far_in[phase, at]
            sum_out(phase, chunk).start()
            sig[at] = inner_out[phase, at] + far_in[phase, at]

    def sum_total(phase, chunk):
        at, _ = sum_place(phase, chunk)

        @pl.when(inner == 0)
        def _():
            sum_swap(phase, chunk).wait_recv()
            sig[at] = part[phase, at] + far_in[phase, at]

    def sum_drain(phase, chunk):
        @pl.when(inner == 0)
        def _():
            sum_in(phase, chunk).wait_send()

        @pl.when(inner == 1)
        def _():
            sum_swap(phase, chunk).wait_send()
            sum_out(phase, chunk).wait_send()

    state["next"] = 2 * 3 * len(CHUNKS)
    chunks = range(len(CHUNKS))
    plain = (((1,), (0,)), ((), ()))
    turned = (((1,), (1,)), ((), ()))

    def encode(chunk):
        at, _ = sum_place(0, chunk)
        part[0, at] = product(acts[at], wenc_h[...], wenc_l[...], plain)
        sum_start(0, chunk)

    def decode(chunk):
        sum_total(0, chunk)
        at, _ = sum_place(0, chunk)
        count = CHUNKS[chunk][1]
        codes, gate = softplus_and_sigmoid(sig[at] + bias[...])
        pg[at] = gate
        high, low = split(codes)
        both = jnp.concatenate([high, low], axis=0)
        for block in range(3):
            cols = slice(block * 768, (block + 1) * 768)
            main = jnp.dot(both, wdec_h[:, cols], preferred_element_type=F32)
            cross = jnp.dot(high, wdec_l[:, cols], preferred_element_type=F32)
            recon[at, cols] = main[:count] + (main[count:] + cross)

    half = 2 * UNIT

    def scatter_near(plane):
        up1 = send(rows(recon, row(plane, 1, 0) + half, half), from_down.at[plane, pl.ds(half, half)], second(1))
        down0 = send(rows(recon, row(plane, 2, 0), half), from_up.at[plane, pl.ds(0, half)], second(-1))
        return up1, down0

    def scatter_far(plane):
        base = row(plane, 3, 0)
        a = send(rows(recon, base, half), far_a.at[plane], second(1))
        b = send(rows(recon, base + half, half), far_b.at[plane], second(-1))
        return a, b

    def scatter_add(plane, copies):
        a, b = copies
        to_up = pl.ds(row(plane, 1, 0), half)
        to_down = pl.ds(row(plane, 2, 0) + half, half)
        a.wait_recv()
        recon[to_up] = recon[to_up] + far_a[plane]
        up0 = send(recon.at[to_up], from_down.at[plane, pl.ds(0, half)], second(1))
        b.wait_recv()
        recon[to_down] = recon[to_down] + far_b[plane]
        down1 = send(recon.at[to_down], from_up.at[plane, pl.ds(half, half)], second(-1))
        return up0, down1

    def scatter_first(plane, copies):
        wait_all(copies)
        row_sum[plane] = recon[pl.ds(row(plane, 0, 0), 4 * UNIT)] + (from_up[plane] + from_down[plane])
        return [
            send(row_sum.at[plane, pl.ds(UNIT, UNIT)], first_in.at[plane, 0], first(1)),
            send(row_sum.at[plane, pl.ds(2 * UNIT, UNIT)], first_in.at[plane, 1], first(-1)),
            send(row_sum.at[plane, pl.ds(3 * UNIT, UNIT)], first_in.at[plane, 2], first(2)),
        ]

    def scatter_total(plane, copies):
        wait_all(copies)
        return row_sum[plane, 0:UNIT] + (first_in[plane, 0] + (first_in[plane, 1] + first_in[plane, 2]))

    def residual(plane, total):
        at = pl.ds(row(plane, 0, 0), UNIT)
        resid[at] = total + bdec_ref[...] - acts[at]

    def code_gradient(chunk):
        at, _ = sum_place(1, chunk)
        part[1, at] = product(resid[at], wdec_h[...], wdec_l[...], turned) + norms[0:1, :]
        sum_start(1, chunk)

    def turn(i, _):
        cols = pl.ds(pl.multiple_of(i * 256, 256), 256)
        for plane in range(2):
            for side, ref in enumerate((acts, acts_sib)):
                to = (plane * 2 + side) * 128
                high, low = split(jnp.transpose(ref[plane * 128 : (plane + 1) * 128, cols]))
                acts_th[cols, to : to + 128] = high
                acts_tl[cols, to : to + 128] = low
        return 0

    gives = {}

    def finish(chunk):
        sum_total(1, chunk)
        at, _ = sum_place(1, chunk)
        pg[at] = pg[at] * sig[at]
        gives[chunk] = send(pg.at[at, pl.ds(256, 256)], pg_in.at[at], sibling)

    def gradient(plane):
        at = slice(plane * 128, (plane + 1) * 128)
        right_h, right_l = split(jnp.concatenate([pg[at, 0:256], pg_in[at, :]], axis=0))
        cols = slice(plane * 256, (plane + 1) * 256)

        def block(i):
            high = acts_th[i * 256 : (i + 1) * 256, cols]
            low = acts_tl[i * 256 : (i + 1) * 256, cols]
            main = jnp.dot(high, right_h, preferred_element_type=F32)
            cross = jnp.dot(high, right_l, preferred_element_type=F32) + jnp.dot(low, right_h, preferred_element_type=F32)
            return main + cross

        return block

    load_acts.wait()
    to_plane, own_first = start_gather(acts)
    load_enc.wait()
    swap_enc = send(wenc.at[0], wenc.at[1], sibling)
    bias[:, 0:256] = benc_ref[0:1, :]
    swap_bias = send(bias.at[:, pl.ds(0, 256)], bias.at[:, pl.ds(256, 256)], sibling)
    split_weights(0)
    wait_all(own_first)
    own_second = gather_second(acts, 0)
    load_dec.wait()
    swap_dec = send(wdec.at[0], wdec.at[1], sibling)
    to_plane.wait_recv()
    other_first = gather_first(acts, 1)
    swap_enc.wait_recv()
    split_weights(1)
    encode(0)
    own_rest = gather_forward(acts, 0, own_second)
    wait_all(other_first)
    other_second = gather_second(acts, 1)
    wait_all(own_rest[:2])
    encode(1)
    sum_middle(0, 0)
    other_rest = gather_forward(acts, 1, other_second)
    wait_all(own_rest[2:])
    encode(2)
    sum_middle(0, 1)
    encode(3)
    sum_relay(0, 0)
    wait_all(other_rest[:2])
    encode(4)
    sum_middle(0, 2)
    sum_relay(0, 1)
    split_decoder(0)
    wait_all(other_rest[2:])
    encode(5)
    sum_middle(0, 3)
    sum_relay(0, 2)
    swap_dec.wait_recv()
    split_decoder(1)
    sum_middle(0, 4)
    swap_bias.wait_recv()
    sum_relay(0, 3)
    sum_middle(0, 5)

    decode(0)
    sum_relay(0, 4)
    decode(1)
    own_near = scatter_near(0)
    decode(2)
    own_far = scatter_far(0)
    sum_relay(0, 5)
    give_acts = send(acts, acts_sib, sibling)
    decode(3)
    decode(4)
    other_near = scatter_near(1)
    own_near = own_near + scatter_add(0, own_far)
    decode(5)
    other_far = scatter_far(1)
    own_scatter = scatter_first(0, own_near)
    other_near = other_near + scatter_add(1, other_far)
    plane_out[0] = scatter_total(0, own_scatter)
    own_to_plane = send(plane_out.at[0], plane_in.at[0], other_plane)
    other_scatter = scatter_first(1, other_near)
    give_acts.wait_recv()
    lax.fori_loop(0, 3, turn, 0)
    other_total = scatter_total(1, other_scatter)
    plane_out[1] = other_total
    other_to_plane = send(plane_out.at[1], plane_in.at[1], other_plane)

    own_to_plane.wait_recv()
    residual(1, other_total + plane_in[0])
    other_first = gather_first(resid, 1)
    lax.fori_loop(3, 9, turn, 0)
    wait_all(other_first)
    other_second = gather_second(resid, 1)
    other_to_plane.wait_recv()
    residual(0, plane_out[0] + plane_in[1])
    own_first = gather_first(resid, 0)
    code_gradient(3)
    other_rest = gather_forward(resid, 1, other_second)
    wait_all(own_first)
    own_second = gather_second(resid, 0)
    wait_all(other_rest[:2])
    code_gradient(4)
    sum_middle(1, 3)
    own_rest = gather_forward(resid, 0, own_second)
    wait_all(other_rest[2:])
    code_gradient(5)
    sum_middle(1, 4)
    code_gradient(0)
    sum_relay(1, 3)
    sum_middle(1, 5)
    wait_all(own_rest[:2])
    code_gradient(1)
    sum_relay(1, 4)
    sum_middle(1, 0)
    wait_all(own_rest[2:])
    code_gradient(2)
    sum_relay(1, 5)
    sum_middle(1, 1)
    sum_relay(1, 0)
    finish(3)
    finish(4)
    sum_middle(1, 2)
    finish(5)
    sum_relay(1, 1)
    finish(0)
    wait_all([gives[3], gives[4], gives[5]])
    block = gradient(1)
    for i in range(9):
        grad_buf[i * 256 : (i + 1) * 256, :] = block(i)
    sum_relay(1, 2)
    finish(1)
    finish(2)
    wait_all([gives[0], gives[1], gives[2]])

    block = gradient(0)
    stores = []
    for i in range(9):
        at = pl.ds(i * 256, 256)
        grad_buf[at, :] = grad_buf[at, :] + block(i)
        store = pltpu.make_async_copy(grad_buf.at[at], grad_hbm.at[0, at], lsem.at[3 + i])
        store.start()
        stores.append(store)
    gbias_ref[...] = jnp.sum(pg[:, 0:256], axis=0, keepdims=True) + jnp.sum(pg_in[...], axis=0, keepdims=True)

    for copy in sent:
        copy.wait_send()
    for phase in range(2):
        for chunk in chunks:
            sum_drain(phase, chunk)
    for store in stores:
        store.wait()


def on_device(acts, w_enc, b_enc, w_dec, b_dec):
    depth = acts.shape[2]
    any_space = pl.BlockSpec(memory_space=pl.ANY)
    vmem = pl.BlockSpec(memory_space=pltpu.VMEM)
    copies = 120
    grad, bias = pl.pallas_call(
        kernel,
        out_shape=(
            jax.ShapeDtypeStruct((1, depth, 256), F32),
            jax.ShapeDtypeStruct((1, 256), F32),
        ),
        in_specs=[any_space, any_space, any_space, vmem, vmem],
        out_specs=(any_space, vmem),
        scratch_shapes=[
            pltpu.VMEM((256, depth), F32),
            pltpu.VMEM((256, depth), F32),
            pltpu.VMEM((256, depth), F32),
            pltpu.VMEM((2, depth, 256), F32),
            pltpu.VMEM((2, 256, depth), F32),
            pltpu.VMEM((depth, 512), BF16),
            pltpu.VMEM((depth, 512), BF16),
            pltpu.VMEM((512, depth), BF16),
            pltpu.VMEM((512, depth), BF16),
            pltpu.VMEM((1, 512), F32),
            pltpu.VMEM((8, 512), F32),
            pltpu.VMEM((256, depth), F32),
            pltpu.VMEM((2, 32, depth), F32),
            pltpu.VMEM((2, 16, depth), F32),
            pltpu.VMEM((2, 16, depth), F32),
            pltpu.VMEM((2, 32, depth), F32),
            pltpu.VMEM((2, 32, depth), F32),
            pltpu.VMEM((2, 3, 8, depth), F32),
            pltpu.VMEM((2, 8, depth), F32),
            pltpu.VMEM((2, 8, depth), F32),
            pltpu.VMEM((2, 256, 512), F32),
            pltpu.VMEM((2, 256, 512), F32),
            pltpu.VMEM((2, 256, 512), F32),
            pltpu.VMEM((2, 256, 512), F32),
            pltpu.VMEM((2, 256, 512), F32),
            pltpu.VMEM((256, 512), F32),
            pltpu.VMEM((256, 512), F32),
            pltpu.VMEM((256, 256), F32),
            pltpu.VMEM((depth, 512), BF16),
            pltpu.VMEM((depth, 512), BF16),
            pltpu.VMEM((depth, 256), F32),
            pltpu.SemaphoreType.DMA((copies,)),
            pltpu.SemaphoreType.DMA((copies,)),
            pltpu.SemaphoreType.DMA((12,)),
        ],
        compiler_params=pltpu.CompilerParams(
            collective_id=0, has_side_effects=True, vmem_limit_bytes=60 * 1024 * 1024
        ),
        cost_estimate=pl.CostEstimate(flops=7_300_000_000, bytes_accessed=10_000_000, transcendentals=500_000),
        name="crosscoder_gradient",
    )(acts, w_enc, w_dec, b_dec, b_enc.reshape(1, 256))
    return grad, bias.reshape(256)


def solution(mesh):
    return jax.shard_map(
        on_device,
        mesh=mesh,
        in_specs=(
            P("layer", "latent", None),
            P("layer", None, "latent"),
            P("latent"),
            P("latent", "layer", None),
            P("layer", None),
        ),
        out_specs=(P("layer", None, "latent"), P("latent")),
        check_vma=False,
    )
```

```python
import functools

import jax
import jax.numpy as jnp
from jax import lax
from jax.experimental import pallas as pl
from jax.experimental.pallas import tpu as pltpu
from jax.sharding import PartitionSpec as P

SHARP = 4.0
MESH = pl.DeviceIdType.MESH
F32 = jnp.float32
BF16 = jnp.bfloat16

STEPS = (0, 1, -1, 2)
UNIT = 8
PIECE = 32
PIECES = 8


def split(value):
    high = value.astype(BF16)
    return high, (value - high.astype(F32)).astype(BF16)


def softplus_and_sigmoid(pre):
    x = SHARP * pre
    e = jnp.exp(-jnp.abs(x))
    codes = (jnp.maximum(x, 0.0) + jnp.log1p(e)) / SHARP
    inv = 1.0 / (1.0 + e)
    return codes, jnp.where(x >= 0, inv, e * inv)


def kernel(
    acts_hbm,
    wenc_hbm,
    wdec_hbm,
    bdec_ref,
    benc_ref,
    grad_hbm,
    gbias_ref,
    acts,
    acts_sib,
    resid,
    wenc,
    wdec,
    wenc_h,
    wenc_l,
    wdec_h,
    wdec_l,
    bias,
    norms,
    recon,
    row_sum,
    far_a,
    far_b,
    from_up,
    from_down,
    first_in,
    plane_out,
    plane_in,
    part,
    near_in,
    inner_out,
    far_in,
    outer_out,
    sig,
    pg,
    pg_in,
    acts_th,
    acts_tl,
    wdec_th,
    wdec_tl,
    grad_buf,
    ssem,
    rsem,
    lsem,
):
    layer = lax.axis_index("layer")
    place = lax.axis_index("latent")
    core = lax.rem(place, 2)
    x = lax.rem(place // 2, 4)
    z_hi = lax.rem(place // 8, 2)
    y = place // 16

    def device(dx, dy, dz, dc):
        nx = lax.rem(x + dx + 4, 4)
        ny = lax.rem(y + dy + 4, 4)
        nz = lax.rem(z_hi + dz, 2)
        nc = lax.rem(core + dc, 2)
        return (layer, ((ny * 2 + nz) * 4 + nx) * 2 + nc)

    def first(d):
        return device(d * (1 - core), d * core, 0, 0)

    def second(d):
        return device(d * core, d * (1 - core), 0, 0)

    other_plane = device(0, 0, 1, 0)
    sibling = device(0, 0, 0, 1)
    upper = layer // 2
    inner = lax.rem(layer + upper, 2)
    toward = 1 - 2 * upper
    far = (layer + toward, place)
    near = (layer - toward, place)

    state = {"next": 0}
    sent = []

    def copy_to(src, dst, target, index=None):
        if index is None:
            index = state["next"]
            state["next"] += 1
        return pltpu.make_async_remote_copy(
            src_ref=src,
            dst_ref=dst,
            send_sem=ssem.at[index],
            recv_sem=rsem.at[index],
            device_id=target,
            device_id_type=MESH,
        )

    def send(src, dst, target):
        copy = copy_to(src, dst, target)
        copy.start()
        sent.append(copy)
        return copy

    load_acts = pltpu.make_async_copy(acts_hbm.at[0], acts.at[pl.ds(0, UNIT)], lsem.at[0])
    load_enc = pltpu.make_async_copy(wenc_hbm.at[0], wenc.at[0], lsem.at[1])
    load_dec = pltpu.make_async_copy(wdec_hbm.at[:, 0], wdec.at[0], lsem.at[2])
    load_acts.start()
    load_enc.start()
    load_dec.start()

    barrier = pltpu.get_barrier_semaphore()
    partners = [first(1), first(-1), first(2), second(1), second(-1), other_plane, sibling, far]
    for partner in partners:
        pl.semaphore_signal(barrier, inc=1, device_id=partner, device_id_type=MESH)

    @pl.when(inner == 1)
    def _():
        pl.semaphore_signal(barrier, inc=1, device_id=near, device_id_type=MESH)

    pl.semaphore_wait(barrier, len(partners) + inner)

    def row(plane, b, a):
        return ((plane * 4 + b) * 4 + a) * UNIT

    def rows(ref, start, count):
        return ref.at[pl.ds(start, count)]

    def gather_first(ref, plane):
        own = rows(ref, row(plane, 0, 0), UNIT)
        return [
            send(own, rows(ref, row(plane, 0, 2), UNIT), first(1)),
            send(own, rows(ref, row(plane, 0, 1), UNIT), first(-1)),
            send(own, rows(ref, row(plane, 0, 3), UNIT), first(2)),
        ]

    def gather_second(ref, plane):
        half = 2 * UNIT
        own = row(plane, 0, 0)
        up = row(plane, 2, 0)
        down = row(plane, 1, 0)
        up0 = send(rows(ref, own, half), rows(ref, up, half), second(1))
        down1 = send(rows(ref, own + half, half), rows(ref, down + half, half), second(-1))
        up1 = send(rows(ref, own + half, half), rows(ref, up + half, half), second(1))
        down0 = send(rows(ref, own, half), rows(ref, down, half), second(-1))
        return up0, down1, up1, down0

    def gather_forward(ref, plane, copies):
        half = 2 * UNIT
        up0, down1, up1, down0 = copies
        last = row(plane, 3, 0)
        up0.wait_recv()
        fwd0 = send(rows(ref, row(plane, 2, 0), half), rows(ref, last, half), second(1))
        down1.wait_recv()
        fwd1 = send(rows(ref, row(plane, 1, 0) + half, half), rows(ref, last + half, half), second(-1))
        return up1, down0, fwd0, fwd1

    def wait_all(copies):
        for copy in copies:
            copy.wait_recv()

    def start_gather(ref):
        to_plane = send(rows(ref, 0, UNIT), rows(ref, row(1, 0, 0), UNIT), other_plane)
        return to_plane, gather_first(ref, 0)

    def split_weights(slot):
        def enc(i, _):
            at = pl.ds(pl.multiple_of(i * 256, 256), 256)
            high, low = split(wenc[slot, at, :])
            wenc_h[at, slot * 256 : (slot + 1) * 256] = high
            wenc_l[at, slot * 256 : (slot + 1) * 256] = low
            return 0

        lax.fori_loop(0, 9, enc, 0)

    def split_decoder(slot):
        def dec(i, _):
            at = pl.ds(pl.multiple_of(i * 32, 32), 32)
            to = pl.ds(pl.multiple_of(slot * 256 + i * 32, 32), 32)
            high, low = split(wdec[slot, at, :])
            wdec_h[to, :] = high
            wdec_l[to, :] = low
            return 0

        lax.fori_loop(0, 8, dec, 0)
        squares = jnp.zeros((256, 128), F32)
        for k in range(wdec.shape[2] // 128):
            value = wdec[slot, :, k * 128 : (k + 1) * 128]
            squares = squares + value * value
        total = lax.dot_general(
            jnp.ones((8, 128), F32),
            squares,
            (((1,), (1,)), ((), ())),
            precision=lax.Precision.HIGHEST,
            preferred_element_type=F32,
        )
        norms[:, slot * 256 : (slot + 1) * 256] = jnp.sqrt(total)

    def product(left, right_h, right_l):
        high, low = split(left)
        count = left.shape[0]
        both = lax.dot_general(jnp.concatenate([high, low], axis=0), right_h, plain, preferred_element_type=F32)
        cross = lax.dot_general(high, right_l, plain, preferred_element_type=F32)
        return both[:count] + (both[count:] + cross)

    def sum_place(phase, chunk):
        return pl.ds(chunk * PIECE, PIECE), (phase * PIECES + chunk) * 3

    def sum_in(phase, chunk):
        at, index = sum_place(phase, chunk)
        return copy_to(part.at[phase, at], near_in.at[phase, at], far, index)

    def sum_swap(phase, chunk):
        at, index = sum_place(phase, chunk)
        return copy_to(inner_out.at[phase, at], far_in.at[phase, at], far, index + 1)

    def sum_out(phase, chunk):
        at, index = sum_place(phase, chunk)
        return pltpu.make_async_remote_copy(
            src_ref=outer_out.at[phase, at],
            dst_ref=far_in.at[phase, at],
            send_sem=ssem.at[index + 2],
            recv_sem=rsem.at[index + 1],
            device_id=near,
            device_id_type=MESH,
        )

    def sum_start(phase, chunk):
        @pl.when(inner == 0)
        def _():
            sum_in(phase, chunk).start()

    def sum_middle(phase, chunk):
        at, _ = sum_place(phase, chunk)

        @pl.when(inner == 1)
        def _():
            sum_in(phase, chunk).wait_recv()
            inner_out[phase, at] = part[phase, at] + near_in[phase, at]
            sum_swap(phase, chunk).start()

    def sum_relay(phase, chunk):
        at, _ = sum_place(phase, chunk)

        @pl.when(inner == 1)
        def _():
            sum_swap(phase, chunk).wait_recv()
            outer_out[phase, at] = part[phase, at] + far_in[phase, at]
            sum_out(phase, chunk).start()
            sig[at] = inner_out[phase, at] + far_in[phase, at]

    def sum_total(phase, chunk):
        at, _ = sum_place(phase, chunk)

        @pl.when(inner == 0)
        def _():
            sum_swap(phase, chunk).wait_recv()
            sig[at] = part[phase, at] + far_in[phase, at]

    def sum_drain(phase, chunk):
        @pl.when(inner == 0)
        def _():
            sum_in(phase, chunk).wait_send()

        @pl.when(inner == 1)
        def _():
            sum_swap(phase, chunk).wait_send()
            sum_out(phase, chunk).wait_send()

    state["next"] = 2 * 3 * PIECES
    chunks = range(PIECES)
    plain = (((1,), (0,)), ((), ()))

    def encode(chunk, pieces):
        at = pl.ds(chunk * PIECE, pieces * PIECE)
        part[0, at] = product(acts[at], wenc_h[...], wenc_l[...])
        for piece in range(chunk, chunk + pieces):
            sum_start(0, piece)

    def decode(chunk, pieces):
        for piece in range(chunk, chunk + pieces):
            sum_total(0, piece)
        count = pieces * PIECE
        at = pl.ds(chunk * PIECE, count)
        codes, gate = softplus_and_sigmoid(sig[at] + bias[...])
        pg[at] = gate
        high, low = split(codes)
        both = jnp.concatenate([high, low], axis=0)
        for block in range(3):
            cols = slice(block * 768, (block + 1) * 768)
            main = jnp.dot(both, wdec_h[:, cols], preferred_element_type=F32)
            cross = jnp.dot(high, wdec_l[:, cols], preferred_element_type=F32)
            recon[at, cols] = main[:count] + (main[count:] + cross)

    half = 2 * UNIT

    def scatter_near(plane):
        up1 = send(rows(recon, row(plane, 1, 0) + half, half), from_down.at[plane, pl.ds(half, half)], second(1))
        down0 = send(rows(recon, row(plane, 2, 0), half), from_up.at[plane, pl.ds(0, half)], second(-1))
        return up1, down0

    def scatter_far(plane):
        base = row(plane, 3, 0)
        a = send(rows(recon, base, half), far_a.at[plane], second(1))
        b = send(rows(recon, base + half, half), far_b.at[plane], second(-1))
        return a, b

    def scatter_add(plane, copies):
        a, b = copies
        to_up = pl.ds(row(plane, 1, 0), half)
        to_down = pl.ds(row(plane, 2, 0) + half, half)
        a.wait_recv()
        recon[to_up] = recon[to_up] + far_a[plane]
        up0 = send(recon.at[to_up], from_down.at[plane, pl.ds(0, half)], second(1))
        b.wait_recv()
        recon[to_down] = recon[to_down] + far_b[plane]
        down1 = send(recon.at[to_down], from_up.at[plane, pl.ds(half, half)], second(-1))
        return up0, down1

    def scatter_first(plane, copies):
        wait_all(copies)
        row_sum[plane] = recon[pl.ds(row(plane, 0, 0), 4 * UNIT)] + (from_up[plane] + from_down[plane])
        return [
            send(row_sum.at[plane, pl.ds(UNIT, UNIT)], first_in.at[plane, 0], first(1)),
            send(row_sum.at[plane, pl.ds(2 * UNIT, UNIT)], first_in.at[plane, 1], first(-1)),
            send(row_sum.at[plane, pl.ds(3 * UNIT, UNIT)], first_in.at[plane, 2], first(2)),
        ]

    def scatter_total(plane, copies):
        wait_all(copies)
        return row_sum[plane, 0:UNIT] + (first_in[plane, 0] + (first_in[plane, 1] + first_in[plane, 2]))

    def residual(plane, total):
        at = pl.ds(row(plane, 0, 0), UNIT)
        resid[at] = total + bdec_ref[...] - acts[at]

    def code_gradient(chunk, pieces):
        at = pl.ds(chunk * PIECE, pieces * PIECE)
        part[1, at] = product(resid[at], wdec_th[...], wdec_tl[...]) + norms[0:1, :]
        for piece in range(chunk, chunk + pieces):
            sum_start(1, piece)

    def turn_decoder(i, _):
        cols = pl.ds(pl.multiple_of(i * 256, 256), 256)
        wdec_th[cols, :] = jnp.transpose(wdec_h[:, cols])
        wdec_tl[cols, :] = jnp.transpose(wdec_l[:, cols])
        return 0

    def turn(i, _):
        cols = pl.ds(pl.multiple_of(i * 256, 256), 256)
        for plane in range(2):
            for side, ref in enumerate((acts, acts_sib)):
                to = (plane * 2 + side) * 128
                high, low = split(jnp.transpose(ref[plane * 128 : (plane + 1) * 128, cols]))
                acts_th[cols, to : to + 128] = high
                acts_tl[cols, to : to + 128] = low
        return 0

    gives = {}

    def finish(chunk):
        sum_total(1, chunk)
        at, _ = sum_place(1, chunk)
        pg[at] = pg[at] * sig[at]
        gives[chunk] = send(pg.at[at, pl.ds(256, 256)], pg_in.at[at], sibling)

    def gradient(plane):
        at = slice(plane * 128, (plane + 1) * 128)
        right_h, right_l = split(jnp.concatenate([pg[at, 0:256], pg_in[at, :]], axis=0))
        cols = slice(plane * 256, (plane + 1) * 256)

        def block(i):
            high = acts_th[i * 256 : (i + 1) * 256, cols]
            low = acts_tl[i * 256 : (i + 1) * 256, cols]
            main = jnp.dot(high, right_h, preferred_element_type=F32)
            cross = jnp.dot(high, right_l, preferred_element_type=F32) + jnp.dot(low, right_h, preferred_element_type=F32)
            return main + cross

        return block

    load_acts.wait()
    to_plane, own_first = start_gather(acts)
    load_enc.wait()
    swap_enc = send(wenc.at[0], wenc.at[1], sibling)
    bias[:, 0:256] = benc_ref[0:1, :]
    swap_bias = send(bias.at[:, pl.ds(0, 256)], bias.at[:, pl.ds(256, 256)], sibling)
    split_weights(0)
    wait_all(own_first)
    to_plane.wait_recv()
    other_first = gather_first(acts, 1)
    own_second = gather_second(acts, 0)
    load_dec.wait()
    swap_dec = send(wdec.at[0], wdec.at[1], sibling)
    swap_enc.wait_recv()
    split_weights(1)
    encode(0, 1)
    own_rest = gather_forward(acts, 0, own_second)
    wait_all(other_first)
    other_second = gather_second(acts, 1)
    wait_all(own_rest[:2])
    encode(1, 2)
    sum_middle(0, 0)
    sum_middle(0, 1)
    other_rest = gather_forward(acts, 1, other_second)
    sum_middle(0, 2)
    wait_all(own_rest[2:])
    encode(3, 1)
    encode(4, 1)
    sum_relay(0, 0)
    wait_all(other_rest[:2])
    encode(5, 2)
    split_decoder(0)
    sum_relay(0, 1)
    sum_middle(0, 3)
    sum_relay(0, 2)
    wait_all(other_rest[2:])
    encode(7, 1)
    give_acts = send(acts, acts_sib, sibling)
    sum_middle(0, 4)
    swap_dec.wait_recv()
    split_decoder(1)
    sum_middle(0, 5)
    sum_middle(0, 6)
    sum_relay(0, 3)
    swap_bias.wait_recv()

    decode(0, 1)
    sum_middle(0, 7)
    sum_relay(0, 4)
    decode(1, 2)
    own_near = scatter_near(0)
    sum_relay(0, 5)
    sum_relay(0, 6)
    decode(3, 1)
    own_far = scatter_far(0)
    sum_relay(0, 7)
    decode(4, 1)
    decode(5, 2)
    other_near = scatter_near(1)
    own_near = own_near + scatter_add(0, own_far)
    decode(7, 1)
    other_far = scatter_far(1)
    lax.fori_loop(0, 9, turn_decoder, 0)
    own_scatter = scatter_first(0, own_near)
    other_near = other_near + scatter_add(1, other_far)
    plane_out[0] = scatter_total(0, own_scatter)
    own_to_plane = send(plane_out.at[0], plane_in.at[0], other_plane)
    other_scatter = scatter_first(1, other_near)
    other_total = scatter_total(1, other_scatter)
    plane_out[1] = other_total
    other_to_plane = send(plane_out.at[1], plane_in.at[1], other_plane)

    own_to_plane.wait_recv()
    residual(1, other_total + plane_in[0])
    other_first = gather_first(resid, 1)
    give_acts.wait_recv()
    lax.fori_loop(0, 9, turn, 0)
    other_to_plane.wait_recv()
    residual(0, plane_out[0] + plane_in[1])
    own_first = gather_first(resid, 0)
    wait_all(other_first)
    other_second = gather_second(resid, 1)
    code_gradient(4, 1)
    other_rest = gather_forward(resid, 1, other_second)
    wait_all(own_first)
    own_second = gather_second(resid, 0)
    wait_all(other_rest[:2])
    code_gradient(5, 2)
    sum_middle(1, 4)
    own_rest = gather_forward(resid, 0, own_second)
    sum_middle(1, 5)
    sum_middle(1, 6)
    wait_all(other_rest[2:])
    code_gradient(7, 1)
    code_gradient(0, 1)
    sum_relay(1, 4)
    wait_all(own_rest[:2])
    code_gradient(1, 2)
    sum_middle(1, 7)
    wait_all(own_rest[2:])
    code_gradient(3, 1)
    sum_middle(1, 0)
    sum_relay(1, 5)
    sum_relay(1, 6)
    sum_middle(1, 1)
    sum_middle(1, 2)
    sum_relay(1, 7)
    sum_middle(1, 3)
    sum_relay(1, 0)
    for chunk in (4, 5, 6, 7):
        finish(chunk)
    sum_relay(1, 1)
    sum_relay(1, 2)
    wait_all([gives[4], gives[5], gives[6], gives[7]])
    block = gradient(1)
    for i in range(9):
        grad_buf[i * 256 : (i + 1) * 256, :] = block(i)
    sum_relay(1, 3)
    for chunk in (0, 1, 2, 3):
        finish(chunk)
    wait_all([gives[0], gives[1], gives[2], gives[3]])

    block = gradient(0)
    stores = []
    for i in range(9):
        at = pl.ds(i * 256, 256)
        grad_buf[at, :] = grad_buf[at, :] + block(i)
        store = pltpu.make_async_copy(grad_buf.at[at], grad_hbm.at[0, at], lsem.at[3 + i])
        store.start()
        stores.append(store)
    gbias_ref[...] = jnp.sum(pg[:, 0:256], axis=0, keepdims=True) + jnp.sum(pg_in[...], axis=0, keepdims=True)

    for copy in sent:
        copy.wait_send()
    for phase in range(2):
        for chunk in chunks:
            sum_drain(phase, chunk)
    for store in stores:
        store.wait()


def on_device(acts, w_enc, b_enc, w_dec, b_dec):
    depth = acts.shape[2]
    any_space = pl.BlockSpec(memory_space=pl.ANY)
    vmem = pl.BlockSpec(memory_space=pltpu.VMEM)
    copies = 140
    grad, bias = pl.pallas_call(
        kernel,
        out_shape=(
            jax.ShapeDtypeStruct((1, depth, 256), F32),
            jax.ShapeDtypeStruct((1, 256), F32),
        ),
        in_specs=[any_space, any_space, any_space, vmem, vmem],
        out_specs=(any_space, vmem),
        scratch_shapes=[
            pltpu.VMEM((256, depth), F32),
            pltpu.VMEM((256, depth), F32),
            pltpu.VMEM((256, depth), F32),
            pltpu.VMEM((2, depth, 256), F32),
            pltpu.VMEM((2, 256, depth), F32),
            pltpu.VMEM((depth, 512), BF16),
            pltpu.VMEM((depth, 512), BF16),
            pltpu.VMEM((512, depth), BF16),
            pltpu.VMEM((512, depth), BF16),
            pltpu.VMEM((1, 512), F32),
            pltpu.VMEM((8, 512), F32),
            pltpu.VMEM((256, depth), F32),
            pltpu.VMEM((2, 32, depth), F32),
            pltpu.VMEM((2, 16, depth), F32),
            pltpu.VMEM((2, 16, depth), F32),
            pltpu.VMEM((2, 32, depth), F32),
            pltpu.VMEM((2, 32, depth), F32),
            pltpu.VMEM((2, 3, 8, depth), F32),
            pltpu.VMEM((2, 8, depth), F32),
            pltpu.VMEM((2, 8, depth), F32),
            pltpu.VMEM((2, 256, 512), F32),
            pltpu.VMEM((2, 256, 512), F32),
            pltpu.VMEM((2, 256, 512), F32),
            pltpu.VMEM((2, 256, 512), F32),
            pltpu.VMEM((2, 256, 512), F32),
            pltpu.VMEM((256, 512), F32),
            pltpu.VMEM((256, 512), F32),
            pltpu.VMEM((256, 256), F32),
            pltpu.VMEM((depth, 512), BF16),
            pltpu.VMEM((depth, 512), BF16),
            pltpu.VMEM((depth, 512), BF16),
            pltpu.VMEM((depth, 512), BF16),
            pltpu.VMEM((depth, 256), F32),
            pltpu.SemaphoreType.DMA((copies,)),
            pltpu.SemaphoreType.DMA((copies,)),
            pltpu.SemaphoreType.DMA((12,)),
        ],
        compiler_params=pltpu.CompilerParams(
            collective_id=0, has_side_effects=True, vmem_limit_bytes=60 * 1024 * 1024
        ),
        cost_estimate=pl.CostEstimate(flops=7_300_000_000, bytes_accessed=10_000_000, transcendentals=500_000),
        name="crosscoder_gradient",
    )(acts, w_enc, w_dec, b_dec, b_enc.reshape(1, 256))
    return grad, bias.reshape(256)


def solution(mesh):
    return jax.shard_map(
        on_device,
        mesh=mesh,
        in_specs=(
            P("layer", "latent", None),
            P("layer", None, "latent"),
            P("latent"),
            P("latent", "layer", None),
            P("layer", None),
        ),
        out_specs=(P("layer", None, "latent"), P("latent")),
        check_vma=False,
    )
```

```python
import functools

import jax
import jax.numpy as jnp
from jax import lax
from jax.experimental import pallas as pl
from jax.experimental.pallas import tpu as pltpu
from jax.sharding import PartitionSpec as P

SHARP = 4.0
MESH = pl.DeviceIdType.MESH
F32 = jnp.float32
BF16 = jnp.bfloat16

STEPS = (0, 1, -1, 2)
UNIT = 8
PIECE = 32
PIECES = 8


def split(value):
    high = value.astype(BF16)
    return high, (value - high.astype(F32)).astype(BF16)


def softplus_and_sigmoid(pre):
    x = SHARP * pre
    e = jnp.exp(-jnp.abs(x))
    codes = (jnp.maximum(x, 0.0) + jnp.log1p(e)) / SHARP
    inv = 1.0 / (1.0 + e)
    return codes, jnp.where(x >= 0, inv, e * inv)


def kernel(
    acts_hbm,
    wenc_hbm,
    wdec_hbm,
    bdec_ref,
    benc_ref,
    done_hbm,
    left_hbm,
    right_ref,
    gbias_ref,
    acts,
    acts_sib,
    resid,
    wenc,
    wdec,
    wenc_h,
    wenc_l,
    wdec_h,
    wdec_l,
    bias,
    norms,
    recon,
    row_sum,
    far_a,
    far_b,
    from_up,
    from_down,
    first_in,
    plane_out,
    plane_in,
    part,
    near_in,
    inner_out,
    far_in,
    outer_out,
    sig,
    pg,
    pg_in,
    acts_th,
    acts_tl,
    wdec_th,
    wdec_tl,
    grad_buf,
    ssem,
    rsem,
    lsem,
):
    layer = lax.axis_index("layer")
    place = lax.axis_index("latent")
    core = lax.rem(place, 2)
    x = lax.rem(place // 2, 4)
    z_hi = lax.rem(place // 8, 2)
    y = place // 16

    def device(dx, dy, dz, dc):
        nx = lax.rem(x + dx + 4, 4)
        ny = lax.rem(y + dy + 4, 4)
        nz = lax.rem(z_hi + dz, 2)
        nc = lax.rem(core + dc, 2)
        return (layer, ((ny * 2 + nz) * 4 + nx) * 2 + nc)

    def first(d):
        return device(d * (1 - core), d * core, 0, 0)

    def second(d):
        return device(d * core, d * (1 - core), 0, 0)

    other_plane = device(0, 0, 1, 0)
    sibling = device(0, 0, 0, 1)
    upper = layer // 2
    inner = lax.rem(layer + upper, 2)
    toward = 1 - 2 * upper
    far = (layer + toward, place)
    near = (layer - toward, place)

    state = {"next": 0}
    sent = []

    def copy_to(src, dst, target, index=None):
        if index is None:
            index = state["next"]
            state["next"] += 1
        return pltpu.make_async_remote_copy(
            src_ref=src,
            dst_ref=dst,
            send_sem=ssem.at[index],
            recv_sem=rsem.at[index],
            device_id=target,
            device_id_type=MESH,
        )

    def send(src, dst, target):
        copy = copy_to(src, dst, target)
        copy.start()
        sent.append(copy)
        return copy

    load_acts = pltpu.make_async_copy(acts_hbm.at[0], acts.at[pl.ds(0, UNIT)], lsem.at[0])
    load_enc = pltpu.make_async_copy(wenc_hbm.at[0], wenc.at[0], lsem.at[1])
    load_dec = pltpu.make_async_copy(wdec_hbm.at[:, 0], wdec.at[0], lsem.at[2])
    load_acts.start()
    load_enc.start()
    load_dec.start()

    barrier = pltpu.get_barrier_semaphore()
    partners = [first(1), first(-1), first(2), second(1), second(-1), other_plane, sibling, far]
    for partner in partners:
        pl.semaphore_signal(barrier, inc=1, device_id=partner, device_id_type=MESH)

    @pl.when(inner == 1)
    def _():
        pl.semaphore_signal(barrier, inc=1, device_id=near, device_id_type=MESH)

    pl.semaphore_wait(barrier, len(partners) + inner)

    def row(plane, b, a):
        return ((plane * 4 + b) * 4 + a) * UNIT

    def rows(ref, start, count):
        return ref.at[pl.ds(start, count)]

    def gather_first(ref, plane):
        own = rows(ref, row(plane, 0, 0), UNIT)
        return [
            send(own, rows(ref, row(plane, 0, 2), UNIT), first(1)),
            send(own, rows(ref, row(plane, 0, 1), UNIT), first(-1)),
            send(own, rows(ref, row(plane, 0, 3), UNIT), first(2)),
        ]

    def gather_second(ref, plane):
        half = 2 * UNIT
        own = row(plane, 0, 0)
        up = row(plane, 2, 0)
        down = row(plane, 1, 0)
        up0 = send(rows(ref, own, half), rows(ref, up, half), second(1))
        down1 = send(rows(ref, own + half, half), rows(ref, down + half, half), second(-1))
        up1 = send(rows(ref, own + half, half), rows(ref, up + half, half), second(1))
        down0 = send(rows(ref, own, half), rows(ref, down, half), second(-1))
        return up0, down1, up1, down0

    def gather_forward(ref, plane, copies):
        half = 2 * UNIT
        up0, down1, up1, down0 = copies
        last = row(plane, 3, 0)
        up0.wait_recv()
        fwd0 = send(rows(ref, row(plane, 2, 0), half), rows(ref, last, half), second(1))
        down1.wait_recv()
        fwd1 = send(rows(ref, row(plane, 1, 0) + half, half), rows(ref, last + half, half), second(-1))
        return up1, down0, fwd0, fwd1

    def wait_all(copies):
        for copy in copies:
            copy.wait_recv()

    def start_gather(ref):
        to_plane = send(rows(ref, 0, UNIT), rows(ref, row(1, 0, 0), UNIT), other_plane)
        return to_plane, gather_first(ref, 0)

    def split_weights(slot):
        def enc(i, _):
            at = pl.ds(pl.multiple_of(i * 256, 256), 256)
            high, low = split(wenc[slot, at, :])
            wenc_h[at, slot * 256 : (slot + 1) * 256] = high
            wenc_l[at, slot * 256 : (slot + 1) * 256] = low
            return 0

        lax.fori_loop(0, 9, enc, 0)

    def split_decoder(slot):
        def dec(i, _):
            at = pl.ds(pl.multiple_of(i * 32, 32), 32)
            to = pl.ds(pl.multiple_of(slot * 256 + i * 32, 32), 32)
            high, low = split(wdec[slot, at, :])
            wdec_h[to, :] = high
            wdec_l[to, :] = low
            return 0

        lax.fori_loop(0, 8, dec, 0)
        squares = jnp.zeros((256, 128), F32)
        for k in range(wdec.shape[2] // 128):
            value = wdec[slot, :, k * 128 : (k + 1) * 128]
            squares = squares + value * value
        total = lax.dot_general(
            jnp.ones((8, 128), F32),
            squares,
            (((1,), (1,)), ((), ())),
            precision=lax.Precision.HIGHEST,
            preferred_element_type=F32,
        )
        norms[:, slot * 256 : (slot + 1) * 256] = jnp.sqrt(total)

    def product(left, right_h, right_l):
        high, low = split(left)
        count = left.shape[0]
        both = lax.dot_general(jnp.concatenate([high, low], axis=0), right_h, plain, preferred_element_type=F32)
        cross = lax.dot_general(high, right_l, plain, preferred_element_type=F32)
        return both[:count] + (both[count:] + cross)

    def sum_place(phase, chunk):
        return pl.ds(chunk * PIECE, PIECE), (phase * PIECES + chunk) * 3

    def sum_in(phase, chunk):
        at, index = sum_place(phase, chunk)
        return copy_to(part.at[phase, at], near_in.at[phase, at], far, index)

    def sum_swap(phase, chunk):
        at, index = sum_place(phase, chunk)
        return copy_to(inner_out.at[phase, at], far_in.at[phase, at], far, index + 1)

    def sum_out(phase, chunk):
        at, index = sum_place(phase, chunk)
        return pltpu.make_async_remote_copy(
            src_ref=outer_out.at[phase, at],
            dst_ref=far_in.at[phase, at],
            send_sem=ssem.at[index + 2],
            recv_sem=rsem.at[index + 1],
            device_id=near,
            device_id_type=MESH,
        )

    def sum_start(phase, chunk):
        @pl.when(inner == 0)
        def _():
            sum_in(phase, chunk).start()

    def sum_middle(phase, chunk):
        at, _ = sum_place(phase, chunk)

        @pl.when(inner == 1)
        def _():
            sum_in(phase, chunk).wait_recv()
            inner_out[phase, at] = part[phase, at] + near_in[phase, at]
            sum_swap(phase, chunk).start()

    def sum_relay(phase, chunk):
        at, _ = sum_place(phase, chunk)

        @pl.when(inner == 1)
        def _():
            sum_swap(phase, chunk).wait_recv()
            outer_out[phase, at] = part[phase, at] + far_in[phase, at]
            sum_out(phase, chunk).start()
            sig[at] = inner_out[phase, at] + far_in[phase, at]

    def sum_total(phase, chunk):
        at, _ = sum_place(phase, chunk)

        @pl.when(inner == 0)
        def _():
            sum_swap(phase, chunk).wait_recv()
            sig[at] = part[phase, at] + far_in[phase, at]

    def sum_drain(phase, chunk):
        @pl.when(inner == 0)
        def _():
            sum_in(phase, chunk).wait_send()

        @pl.when(inner == 1)
        def _():
            sum_swap(phase, chunk).wait_send()
            sum_out(phase, chunk).wait_send()

    state["next"] = 2 * 3 * PIECES
    chunks = range(PIECES)
    plain = (((1,), (0,)), ((), ()))

    def encode(chunk, pieces):
        at = pl.ds(chunk * PIECE, pieces * PIECE)
        part[0, at] = product(acts[at], wenc_h[...], wenc_l[...])
        for piece in range(chunk, chunk + pieces):
            sum_start(0, piece)

    def decode(chunk, pieces):
        for piece in range(chunk, chunk + pieces):
            sum_total(0, piece)
        count = pieces * PIECE
        at = pl.ds(chunk * PIECE, count)
        codes, gate = softplus_and_sigmoid(sig[at] + bias[...])
        pg[at] = gate
        high, low = split(codes)
        both = jnp.concatenate([high, low], axis=0)
        for block in range(3):
            cols = slice(block * 768, (block + 1) * 768)
            main = jnp.dot(both, wdec_h[:, cols], preferred_element_type=F32)
            cross = jnp.dot(high, wdec_l[:, cols], preferred_element_type=F32)
            recon[at, cols] = main[:count] + (main[count:] + cross)

    half = 2 * UNIT

    def scatter_near(plane):
        up1 = send(rows(recon, row(plane, 1, 0) + half, half), from_down.at[plane, pl.ds(half, half)], second(1))
        down0 = send(rows(recon, row(plane, 2, 0), half), from_up.at[plane, pl.ds(0, half)], second(-1))
        return up1, down0

    def scatter_far(plane):
        base = row(plane, 3, 0)
        a = send(rows(recon, base, half), far_a.at[plane], second(1))
        b = send(rows(recon, base + half, half), far_b.at[plane], second(-1))
        return a, b

    def scatter_add(plane, copies):
        a, b = copies
        to_up = pl.ds(row(plane, 1, 0), half)
        to_down = pl.ds(row(plane, 2, 0) + half, half)
        a.wait_recv()
        recon[to_up] = recon[to_up] + far_a[plane]
        up0 = send(recon.at[to_up], from_down.at[plane, pl.ds(0, half)], second(1))
        b.wait_recv()
        recon[to_down] = recon[to_down] + far_b[plane]
        down1 = send(recon.at[to_down], from_up.at[plane, pl.ds(half, half)], second(-1))
        return up0, down1

    def scatter_first(plane, copies):
        wait_all(copies)
        row_sum[plane] = recon[pl.ds(row(plane, 0, 0), 4 * UNIT)] + (from_up[plane] + from_down[plane])
        return [
            send(row_sum.at[plane, pl.ds(UNIT, UNIT)], first_in.at[plane, 0], first(1)),
            send(row_sum.at[plane, pl.ds(2 * UNIT, UNIT)], first_in.at[plane, 1], first(-1)),
            send(row_sum.at[plane, pl.ds(3 * UNIT, UNIT)], first_in.at[plane, 2], first(2)),
        ]

    def scatter_total(plane, copies):
        wait_all(copies)
        return row_sum[plane, 0:UNIT] + (first_in[plane, 0] + (first_in[plane, 1] + first_in[plane, 2]))

    def residual(plane, total):
        at = pl.ds(row(plane, 0, 0), UNIT)
        resid[at] = total + bdec_ref[...] - acts[at]

    def code_gradient(chunk, pieces):
        at = pl.ds(chunk * PIECE, pieces * PIECE)
        part[1, at] = product(resid[at], wdec_th[...], wdec_tl[...]) + norms[0:1, :]
        for piece in range(chunk, chunk + pieces):
            sum_start(1, piece)

    def turn_decoder(i, _):
        cols = pl.ds(pl.multiple_of(i * 256, 256), 256)
        wdec_th[cols, :] = jnp.transpose(wdec_h[:, cols])
        wdec_tl[cols, :] = jnp.transpose(wdec_l[:, cols])
        return 0

    def turn(i, _):
        cols = pl.ds(pl.multiple_of(i * 256, 256), 256)
        for side, ref in enumerate((acts, acts_sib)):
            high, low = split(jnp.transpose(ref[128:256, cols]))
            acts_th[cols, side * 128 : (side + 1) * 128] = high
            acts_tl[cols, side * 128 : (side + 1) * 128] = low
        return 0

    gives = {}

    def finish(chunk):
        sum_total(1, chunk)
        at, _ = sum_place(1, chunk)
        pg[at] = pg[at] * sig[at]
        gives[chunk] = send(pg.at[at, pl.ds(256, 256)], pg_in.at[at], sibling)

    load_acts.wait()
    to_plane, own_first = start_gather(acts)
    load_enc.wait()
    swap_enc = send(wenc.at[0], wenc.at[1], sibling)
    bias[:, 0:256] = benc_ref[0:1, :]
    swap_bias = send(bias.at[:, pl.ds(0, 256)], bias.at[:, pl.ds(256, 256)], sibling)
    split_weights(0)
    wait_all(own_first)
    to_plane.wait_recv()
    other_first = gather_first(acts, 1)
    own_second = gather_second(acts, 0)
    load_dec.wait()
    swap_dec = send(wdec.at[0], wdec.at[1], sibling)
    swap_enc.wait_recv()
    split_weights(1)
    encode(0, 1)
    own_rest = gather_forward(acts, 0, own_second)
    wait_all(other_first)
    other_second = gather_second(acts, 1)
    wait_all(own_rest[:2])
    encode(1, 2)
    sum_middle(0, 0)
    sum_middle(0, 1)
    other_rest = gather_forward(acts, 1, other_second)
    sum_middle(0, 2)
    wait_all(own_rest[2:])
    encode(3, 1)
    encode(4, 1)
    sum_relay(0, 0)
    wait_all(other_rest[:2])
    encode(5, 2)
    split_decoder(0)
    sum_relay(0, 1)
    sum_middle(0, 3)
    sum_relay(0, 2)
    wait_all(other_rest[2:])
    encode(7, 1)
    give_acts = send(acts, acts_sib, sibling)
    sum_middle(0, 4)
    swap_dec.wait_recv()
    split_decoder(1)
    sum_middle(0, 5)
    sum_middle(0, 6)
    sum_relay(0, 3)
    swap_bias.wait_recv()

    decode(0, 1)
    sum_middle(0, 7)
    sum_relay(0, 4)
    decode(1, 2)
    own_near = scatter_near(0)
    sum_relay(0, 5)
    sum_relay(0, 6)
    decode(3, 1)
    own_far = scatter_far(0)
    sum_relay(0, 7)
    decode(4, 1)
    decode(5, 2)
    other_near = scatter_near(1)
    own_near = own_near + scatter_add(0, own_far)
    decode(7, 1)
    other_far = scatter_far(1)
    lax.fori_loop(0, 9, turn_decoder, 0)
    own_scatter = scatter_first(0, own_near)
    other_near = other_near + scatter_add(1, other_far)
    plane_out[0] = scatter_total(0, own_scatter)
    own_to_plane = send(plane_out.at[0], plane_in.at[0], other_plane)
    other_scatter = scatter_first(1, other_near)
    other_total = scatter_total(1, other_scatter)
    plane_out[1] = other_total
    other_to_plane = send(plane_out.at[1], plane_in.at[1], other_plane)

    own_to_plane.wait_recv()
    residual(1, other_total + plane_in[0])
    other_first = gather_first(resid, 1)
    give_acts.wait_recv()
    lax.fori_loop(0, 9, turn, 0)
    other_to_plane.wait_recv()
    residual(0, plane_out[0] + plane_in[1])
    own_first = gather_first(resid, 0)
    wait_all(other_first)
    other_second = gather_second(resid, 1)
    code_gradient(4, 1)
    other_rest = gather_forward(resid, 1, other_second)
    wait_all(own_first)
    own_second = gather_second(resid, 0)
    wait_all(other_rest[:2])
    code_gradient(5, 2)
    sum_middle(1, 4)
    own_rest = gather_forward(resid, 0, own_second)
    sum_middle(1, 5)
    sum_middle(1, 6)
    wait_all(other_rest[2:])
    code_gradient(7, 1)
    code_gradient(0, 1)
    sum_relay(1, 4)
    wait_all(own_rest[:2])
    code_gradient(1, 2)
    sum_middle(1, 7)
    wait_all(own_rest[2:])
    code_gradient(3, 1)
    sum_middle(1, 0)
    sum_relay(1, 5)
    sum_relay(1, 6)
    sum_middle(1, 1)
    sum_middle(1, 2)
    sum_relay(1, 7)
    sum_middle(1, 3)
    sum_relay(1, 0)
    for chunk in (4, 5, 6, 7):
        finish(chunk)
    sum_relay(1, 1)
    sum_relay(1, 2)
    stores = []

    def store(src, dst):
        copy = pltpu.make_async_copy(src, dst, lsem.at[3 + len(stores)])
        copy.start()
        stores.append(copy)

    store(acts.at[pl.ds(0, 128)], left_hbm.at[pl.ds(0, 128)])
    store(acts_sib.at[pl.ds(0, 128)], left_hbm.at[pl.ds(128, 128)])
    wait_all([gives[4], gives[5], gives[6], gives[7]])
    right_h, right_l = split(jnp.concatenate([pg[128:256, 0:256], pg_in[128:256, :]], axis=0))
    for i in range(9):
        at = pl.ds(i * 256, 256)
        high = acts_th[at, :]
        cross = jnp.dot(high, right_l, preferred_element_type=F32) + jnp.dot(
            acts_tl[at, :], right_h, preferred_element_type=F32
        )
        grad_buf[at, :] = jnp.dot(high, right_h, preferred_element_type=F32) + cross
        store(grad_buf.at[at], done_hbm.at[at])
    sum_relay(1, 3)
    for chunk in (0, 1, 2, 3):
        finish(chunk)
    right_ref[0:128, :] = pg[0:128, 0:256]
    part_bias = jnp.sum(pg[:, 0:256], axis=0, keepdims=True) + jnp.sum(pg_in[128:256, :], axis=0, keepdims=True)
    wait_all([gives[0], gives[1], gives[2], gives[3]])
    right_ref[128:256, :] = pg_in[0:128, :]
    gbias_ref[...] = part_bias + jnp.sum(pg_in[0:128, :], axis=0, keepdims=True)

    for copy in sent:
        copy.wait_send()
    for phase in range(2):
        for chunk in chunks:
            sum_drain(phase, chunk)
    for store in stores:
        store.wait()


def last_kernel(
    done_hbm, left_hbm, right_hbm, bias_hbm, grad_hbm, gbias_hbm, done, left, right, bias, grad, sem_in, sem_out
):
    pieces = 3
    width = left.shape[1] // pieces

    def load(src, dst, index):
        copy = pltpu.make_async_copy(src, dst, sem_in.at[index])
        copy.start()
        return copy

    load_right = load(right_hbm, right, 0)
    loads = []
    for i in range(pieces):
        at = pl.ds(i * width, width)
        loads.append(
            (
                load(left_hbm.at[:, at], left.at[:, at], 2 + i),
                load(done_hbm.at[at], done.at[at], 2 + pieces + i),
            )
        )
    load_bias = load(bias_hbm, bias, 1)
    load_right.wait()
    right_h, right_l = split(right[...])
    dims = (((0,), (0,)), ((), ()))
    stores = []
    for i in range(pieces):
        loads[i][0].wait()
        loads[i][1].wait()
        for k in range(i * width, (i + 1) * width, 256):
            cols = slice(k, k + 256)
            high, low = split(left[:, cols])
            cross = lax.dot_general(high, right_l, dims, preferred_element_type=F32) + lax.dot_general(
                low, right_h, dims, preferred_element_type=F32
            )
            main = lax.dot_general(high, right_h, dims, preferred_element_type=F32)
            grad[cols, :] = done[cols, :] + (main + cross)
            at = pl.ds(k, 256)
            store = pltpu.make_async_copy(grad.at[at], grad_hbm.at[0, at], sem_out.at[len(stores)])
            store.start()
            stores.append(store)
    load_bias.wait()
    store = pltpu.make_async_copy(bias, gbias_hbm, sem_out.at[len(stores)])
    store.start()
    stores.append(store)
    for store in stores:
        store.wait()


def on_device(acts, w_enc, b_enc, w_dec, b_dec):
    depth = acts.shape[2]
    any_space = pl.BlockSpec(memory_space=pl.ANY)
    vmem = pl.BlockSpec(memory_space=pltpu.VMEM)
    copies = 140
    done, left, right, bias = pl.pallas_call(
        kernel,
        out_shape=(
            jax.ShapeDtypeStruct((depth, 256), F32),
            jax.ShapeDtypeStruct((256, depth), F32),
            jax.ShapeDtypeStruct((256, 256), F32),
            jax.ShapeDtypeStruct((1, 256), F32),
        ),
        in_specs=[any_space, any_space, any_space, vmem, vmem],
        out_specs=(any_space, any_space, vmem, vmem),
        scratch_shapes=[
            pltpu.VMEM((256, depth), F32),
            pltpu.VMEM((256, depth), F32),
            pltpu.VMEM((256, depth), F32),
            pltpu.VMEM((2, depth, 256), F32),
            pltpu.VMEM((2, 256, depth), F32),
            pltpu.VMEM((depth, 512), BF16),
            pltpu.VMEM((depth, 512), BF16),
            pltpu.VMEM((512, depth), BF16),
            pltpu.VMEM((512, depth), BF16),
            pltpu.VMEM((1, 512), F32),
            pltpu.VMEM((8, 512), F32),
            pltpu.VMEM((256, depth), F32),
            pltpu.VMEM((2, 32, depth), F32),
            pltpu.VMEM((2, 16, depth), F32),
            pltpu.VMEM((2, 16, depth), F32),
            pltpu.VMEM((2, 32, depth), F32),
            pltpu.VMEM((2, 32, depth), F32),
            pltpu.VMEM((2, 3, 8, depth), F32),
            pltpu.VMEM((2, 8, depth), F32),
            pltpu.VMEM((2, 8, depth), F32),
            pltpu.VMEM((2, 256, 512), F32),
            pltpu.VMEM((2, 256, 512), F32),
            pltpu.VMEM((2, 256, 512), F32),
            pltpu.VMEM((2, 256, 512), F32),
            pltpu.VMEM((2, 256, 512), F32),
            pltpu.VMEM((256, 512), F32),
            pltpu.VMEM((256, 512), F32),
            pltpu.VMEM((256, 256), F32),
            pltpu.VMEM((depth, 256), BF16),
            pltpu.VMEM((depth, 256), BF16),
            pltpu.VMEM((depth, 512), BF16),
            pltpu.VMEM((depth, 512), BF16),
            pltpu.VMEM((depth, 256), F32),
            pltpu.SemaphoreType.DMA((copies,)),
            pltpu.SemaphoreType.DMA((copies,)),
            pltpu.SemaphoreType.DMA((16,)),
        ],
        compiler_params=pltpu.CompilerParams(
            collective_id=0, has_side_effects=True, vmem_limit_bytes=60 * 1024 * 1024
        ),
        cost_estimate=pl.CostEstimate(flops=7_300_000_000, bytes_accessed=10_000_000, transcendentals=500_000),
        name="crosscoder_gradient",
    )(acts, w_enc, w_dec, b_dec, b_enc.reshape(1, 256))
    grad, bias = pl.pallas_call(
        last_kernel,
        out_shape=(
            jax.ShapeDtypeStruct((1, depth, 256), F32),
            jax.ShapeDtypeStruct((1, 256), F32),
        ),
        in_specs=[any_space] * 4,
        out_specs=(any_space, any_space),
        scratch_shapes=[
            pltpu.VMEM((depth, 256), F32),
            pltpu.VMEM((256, depth), F32),
            pltpu.VMEM((256, 256), F32),
            pltpu.VMEM((1, 256), F32),
            pltpu.VMEM((depth, 256), F32),
            pltpu.SemaphoreType.DMA((8,)),
            pltpu.SemaphoreType.DMA((10,)),
        ],
        compiler_params=pltpu.CompilerParams(vmem_limit_bytes=60 * 1024 * 1024),
        cost_estimate=pl.CostEstimate(flops=906_000_000, bytes_accessed=7_400_000, transcendentals=0),
        name="last_product",
    )(done, left, right, bias)
    return grad, bias.reshape(256)


def solution(mesh):
    return jax.shard_map(
        on_device,
        mesh=mesh,
        in_specs=(
            P("layer", "latent", None),
            P("layer", None, "latent"),
            P("latent"),
            P("latent", "layer", None),
            P("layer", None),
        ),
        out_specs=(P("layer", None, "latent"), P("latent")),
        check_vma=False,
    )
```
